256 devices in a mesh: group: 4 (over y), member: 64 (over x, z, core).
Axes of the slice: x: 4, y: 4, z: 8, core: 2. Of those that a mesh axis runs over, the one named last changes fastest.
Arguments:
- embeddings: bfloat16 [8192, 39, 128], P(('group', 'member')), may hold values from -6 to 6
- cot_first: bfloat16 [8192, 100], P(('group', 'member')), may hold values from -6 to 6
- cot_second: bfloat16 [8192, 100], P(('group', 'member')), may hold values from -6 to 6
- cot_third: bfloat16 [8192, 100], P(('group', 'member')), may hold values from -6 to 6
- w_first: bfloat16 [100, 39, 39], replicated, may hold values from -0.15625 to 0.15625
- w_second: bfloat16 [100, 100, 39], replicated, may hold values from -0.09375 to 0.09375
- w_third: bfloat16 [100, 100, 39], replicated, may hold values from -0.09375 to 0.09375
- unique_ids: int32 [256, 768], P(('group', 'member')), may hold values from 0 to 1048575, as said below
- inverse: int32 [8192, 39], P(('group', 'member')), may hold values from 0 to 767, as said below
- table: float32 [1048576, 128], P(('group', 'member')), may hold values from -6 to 6
- accum: float32 [1048576], P(('group', 'member')), may hold values from 1 to 300
- next_ids: int32 [256, 1536], P(('group', 'member')), may hold values from 0 to 1048575, as said below
Outputs:
- new_table: float32 [1048576, 128], P(('group', 'member'))
- new_accum: float32 [1048576], P(('group', 'member'))
- returned: float32 [256, 1536, 128], P(('group', 'member'))
The draws below stay inside these ranges and needn't reach their ends.
Inputs may be any that keep to these rules, and one draw needn't show every extreme that they name: `unique_ids`: row s lists 768 distinct table rows looked up by the samples of device s along group+member, ordered so that the owner r // 4096 never falls; at most 4 rows of one list have the same owner. `inverse`: lookup (n, f) names a position in row n // 32 of unique_ids; every position of a row is named by some lookup. `next_ids`: row s lists 1536 distinct table rows read by device s, ordered so that the owner r // 4096 never falls; at most 8 rows of one list have the same owner.
All inputs are finite; a program needn't handle non-finite values.
Results may differ from the reference program's by a relative error of at most 0.0007.
Values sent between devices are 32-bit elements; how exact they have to be, the bound alone decides.
A program may use at most 64 MiB of HBM per device.

```python
import math
import jax
import jax.numpy as jnp
from jax import lax

FIELDS = 39
EMBED = 128
MAPS = 100
B_DEV = 32
ROWS_DEV = 4096
CAP = 4
RCAP = 8
SAMPLES = 8192
TABLE_ROWS = 1048576
UNIQ = 768
NEXTQ = 1536
N_GROUP = 4
N_MEMBER = 64


def bucketed_rows(key, capacity, length):
    devices = N_GROUP * N_MEMBER
    pair_count = devices * capacity
    hot_key, perm_key = jax.random.split(key)
    hottest = jax.random.randint(hot_key, (), 0, devices)

    def one_list(list_key):
        ranking_key, anchor_key = jax.random.split(list_key)
        ranking = jax.random.permutation(ranking_key, pair_count).astype(jnp.int32)
        indices = jnp.arange(pair_count, dtype=jnp.int32)
        owner_of = indices // capacity
        scores = jnp.where(owner_of == hottest, indices % capacity - pair_count, ranking)
        chosen = jnp.sort(jnp.argsort(scores)[:length].astype(jnp.int32) // capacity)
        leading = jnp.searchsorted(chosen, chosen, side='left').astype(jnp.int32)
        within = jnp.arange(length, dtype=jnp.int32) - leading
        anchor = jax.random.randint(anchor_key, (devices,), 0, ROWS_DEV)
        inside = (anchor[chosen] + within * (ROWS_DEV // capacity)) % ROWS_DEV
        return chosen * ROWS_DEV + inside
    return jax.vmap(one_list)(jax.random.split(perm_key, devices))


def draw_unique_ids(key, part):
    return bucketed_rows(jax.random.fold_in(key, 17), CAP, UNIQ)


def draw_next_ids(key, part):
    return bucketed_rows(jax.random.fold_in(key, 29), RCAP, NEXTQ)


def draw_inverse(key, part):
    devices = N_GROUP * N_MEMBER
    lookups = B_DEV * FIELDS

    def one_list(list_key):
        repeat_key, shuffle_key = jax.random.split(list_key)
        repeats = jax.random.randint(repeat_key, (lookups - UNIQ,), 0, UNIQ)
        complete = jnp.concatenate([jnp.arange(UNIQ, dtype=jnp.int32), repeats.astype(jnp.int32)])
        return jax.random.permutation(shuffle_key, complete)
    lists = jax.vmap(one_list)(jax.random.split(jax.random.fold_in(key, 41), devices))
    return lists.reshape(devices * B_DEV, FIELDS)


def block_scale(rng, extent, cuts, low, top_value):
    gain = 1.0
    for dim, blocks in cuts:
        draws = jax.random.uniform(jax.random.fold_in(jax.random.fold_in(rng, 6), dim), (blocks,), jnp.float32, low / len(cuts), top_value / len(cuts))
        gain = gain * jnp.repeat(jnp.exp(draws), extent[dim] // blocks).reshape((-1,) + (1,) * (len(extent) - 1 - dim))
    return gain


def bell_draw(key, extent, spread, reach, cuts=(), kind=jnp.bfloat16):
    drawn = spread * jax.random.normal(key, extent, jnp.float32)
    if cuts:
        drawn = drawn * block_scale(key, extent, cuts, -0.22, 0.18)
    return jnp.clip(drawn, -reach, reach).astype(kind)


def setup_inputs(seed: int = 0) -> dict:
    keys = jax.random.split(jax.random.key(seed), 13)
    embeddings = bell_draw(keys[0], (SAMPLES, FIELDS, EMBED), 1.0, 6.0, ((0, 256),))
    cot_first = bell_draw(keys[1], (SAMPLES, MAPS), 1.0, 6.0, ((0, 256),))
    cot_second = bell_draw(keys[2], (SAMPLES, MAPS), 1.0, 6.0, ((0, 256),))
    cot_third = bell_draw(keys[3], (SAMPLES, MAPS), 1.0, 6.0, ((0, 256),))
    w_first = bell_draw(keys[4], (MAPS, FIELDS, FIELDS), (FIELDS * FIELDS) ** -0.5, 0.15625)
    w_second = bell_draw(keys[5], (MAPS, MAPS, FIELDS), (MAPS * FIELDS) ** -0.5, 0.09375)
    w_third = bell_draw(keys[6], (MAPS, MAPS, FIELDS), (MAPS * FIELDS) ** -0.5, 0.09375)
    unique_ids = draw_unique_ids(jax.random.fold_in(keys[12], 71), 0)
    inverse = draw_inverse(jax.random.fold_in(keys[12], 71), 0)
    table = bell_draw(keys[9], (TABLE_ROWS, EMBED), 1.0, 6.0, ((0, 256),), jnp.float32)
    accum = jnp.clip(jnp.exp(math.log(300.0) - 5.7037825 * jax.random.uniform(keys[10], (TABLE_ROWS,), jnp.float32) ** block_scale(keys[10], (TABLE_ROWS,), ((0, 256),), -0.2, 0.2)), 1.0, 300.0)
    next_ids = draw_next_ids(jax.random.fold_in(keys[12], 71), 0)
    return dict(embeddings=embeddings, cot_first=cot_first, cot_second=cot_second, cot_third=cot_third, w_first=w_first, w_second=w_second, w_third=w_third, unique_ids=unique_ids, inverse=inverse, table=table, accum=accum, next_ids=next_ids)


RATE = 0.5
EPS = 1e-08

def cin_block(inputs, first_cot, second_cot, third_cot, first_w, second_w, third_w):
    exact = lax.Precision.HIGHEST
    widened = inputs.astype(jnp.float32)
    pairs_one = (widened[:, :, None] * widened[:, None]).astype(jnp.bfloat16)
    layer_one = jnp.einsum('hij,nijd->nhd', first_w.astype(jnp.float32), pairs_one.astype(jnp.float32)).astype(jnp.bfloat16)
    one_wide = layer_one.astype(jnp.float32)
    pairs_two = (one_wide[:, :, None] * widened[:, None]).astype(jnp.bfloat16)
    layer_two = jnp.einsum('hij,nijd->nhd', second_w.astype(jnp.float32), pairs_two.astype(jnp.float32)).astype(jnp.bfloat16)
    two_wide = layer_two.astype(jnp.float32)
    top_map = jnp.einsum('hij,nh->nij', third_w.astype(jnp.float32), third_cot.astype(jnp.float32))
    grad_two = jnp.einsum('nij,njd->nid', top_map, widened, precision=exact)
    grad_base = jnp.einsum('nij,nid->njd', top_map, two_wide, precision=exact)
    upper = (second_cot.astype(jnp.float32)[:, :, None] + grad_two).astype(jnp.bfloat16)
    middle = jnp.einsum('hij,nhd->nijd', second_w.astype(jnp.float32), upper.astype(jnp.float32))
    grad_one = lax.optimization_barrier(jnp.sum(middle * widened[:, None], axis=2))
    grad_base = grad_base + lax.optimization_barrier(jnp.sum(middle * one_wide[:, :, None], axis=1))
    lower = (first_cot.astype(jnp.float32)[:, :, None] + grad_one).astype(jnp.bfloat16)
    bottom = jnp.einsum('hij,nhd->nijd', first_w.astype(jnp.float32), lower.astype(jnp.float32))
    grad_base = grad_base + lax.optimization_barrier(jnp.sum(bottom * widened[:, None], axis=2)) + lax.optimization_barrier(jnp.sum(bottom * widened[:, :, None], axis=1))
    return grad_base

def reference(embeddings, cot_first, cot_second, cot_third, w_first, w_second, w_third, unique_ids, inverse, table, accum, next_ids):
    devices = N_GROUP * N_MEMBER

    def one_device(pieces):
        return cin_block(pieces[0], pieces[1], pieces[2], pieces[3], w_first, w_second, w_third)
    pieces = (embeddings.reshape(devices, B_DEV, FIELDS, EMBED), cot_first.reshape(devices, B_DEV, MAPS), cot_second.reshape(devices, B_DEV, MAPS), cot_third.reshape(devices, B_DEV, MAPS))
    grads = lax.map(one_device, pieces)
    row_ids = jnp.take_along_axis(unique_ids, inverse.reshape(devices, B_DEV * FIELDS), axis=1)
    table_grad = jax.ops.segment_sum(grads.reshape(-1, EMBED), row_ids.reshape(-1), num_segments=TABLE_ROWS)
    new_accum = accum + lax.optimization_barrier(jnp.mean(table_grad * table_grad, axis=1))
    new_table = table - RATE * table_grad / (jnp.sqrt(new_accum) + EPS)[:, None]
    returned = jnp.take(new_table, next_ids, axis=0)
    return (new_table, new_accum, returned)
```

```python
import jax
import jax.numpy as jnp
from jax import lax
from jax.experimental import pallas as pl
from jax.experimental.pallas import tpu as pltpu
from jax.sharding import PartitionSpec as P

CAP = 4
RCAP = 8
RATE = 0.5
EPS = 1e-08

BF = jnp.bfloat16
F32 = jnp.float32


def halves(x):
    hi = x.astype(BF)
    return hi, (x - hi.astype(F32)).astype(BF)


def dot(a, b):
    return jnp.dot(a, b, preferred_element_type=F32)


FP = 48
FQ = 40
HP = 112
HQ = 104
KP = 128
JC = 3


def cin_kernel(
    fields,
    e_ref, c1_ref, c2_ref, thi_ref, tlo_ref, uhi_ref, ulo_ref,
    w1f_ref, w2f_ref, w2b_ref, w1b_ref,
    out_ref,
    ef, p1, p2, l1f, mid, bot, part, l2s,
):
    lanes = 256
    e = jnp.concatenate([e_ref[0], e_ref[1]], axis=1)
    ef[...] = e.astype(F32)
    e3 = e.reshape(FP // 16, 16, lanes)

    def row16(i):
        return jnp.broadcast_to(ef[i : i + 1, :], (16, lanes)).astype(BF)

    uppers = []
    for s in range(2):
        grad_two = dot(thi_ref[s], e_ref[s]) + dot(tlo_ref[s], e_ref[s])
        uppers.append((c2_ref[0, :, s : s + 1] + grad_two).astype(BF))
    upper = jnp.concatenate(uppers, axis=1)
    upper = jnp.concatenate([upper, jnp.zeros((KP - HP, lanes), BF)], axis=0)

    for i in range(fields):
        p1[i * FP : (i + 1) * FP, :] = (e3 * row16(i)[None]).reshape(FP, lanes)
    l1 = dot(w1f_ref[...], p1[...]).astype(BF)
    l1f[...] = l1.astype(F32)
    l3 = l1.reshape(HP // 16, 16, lanes)

    acc = [jnp.zeros((HQ // 8, 8, 128), F32) for _ in range(2)]
    done = 0
    l2 = None
    for c in range(fields // JC):
        mid[c % 2] = dot(w2b_ref[c * JC * HP : (c + 1) * JC * HP, :], upper)
        for k in range(JC):
            j = c * JC + k
            p2[j * HP : (j + 1) * HP, :] = (l3 * row16(j)[None]).reshape(HP, lanes)
        ready = (c + 1) * JC * HP
        if c + 1 < fields // JC:
            ready = ready // 512 * 512
        if ready > done:
            piece = dot(w2f_ref[:, done:ready], p2[done:ready, :])
            if done:
                piece = piece + l2s[...]
            l2s[...] = piece
            done = ready
        for s in range(2):
            ls = slice(s * 128, (s + 1) * 128)
            one = l1f[:HQ, ls].reshape(HQ // 8, 8, 128)
            for k in range(JC):
                j = c * JC + k
                m = mid[c % 2, k * HP : k * HP + HQ, ls].reshape(HQ // 8, 8, 128)
                b = jnp.broadcast_to(ef[j : j + 1, ls], (8, 128))
                acc[s] = acc[s] + m * b[None]
                part[j, :, ls] = jnp.sum(m * one, axis=0)
    l2 = l2s[...].astype(BF)
    bases = [
        dot(uhi_ref[s], l2[:, s * 128 : (s + 1) * 128]) + dot(ulo_ref[s], l2[:, s * 128 : (s + 1) * 128])
        for s in range(2)
    ]
    lower = jnp.concatenate(
        [(c1_ref[0, :HQ, s : s + 1] + acc[s].reshape(HQ, 128)).astype(F32) for s in range(2)], axis=1
    )
    lower = jnp.concatenate([lower, jnp.zeros((KP - HQ, lanes), F32)], axis=0).astype(BF)
    lower = jnp.concatenate([lower, lower], axis=0)
    for c in range(FQ // 8):
        buf = c % 2
        bot[buf] = dot(w1b_ref[c * 8 * FQ : (c + 1) * 8 * FQ, :], lower)
        for s in range(2):
            ls = slice(s * 128, (s + 1) * 128)
            es = ef[:FQ, ls].reshape(FQ // 8, 8, 128)
            for k in range(8):
                j = c * 8 + k
                m = bot[buf, k * FQ : (k + 1) * FQ, ls].reshape(FQ // 8, 8, 128)
                t = jnp.sum(m * es, axis=0)
                if j < fields:
                    t = t + part[j, :, ls]
                part[j, :, ls] = t
    for s in range(2):
        ls = slice(s * 128, (s + 1) * 128)
        out_ref[s] = jnp.sum(part[:, :, ls], axis=1) + bases[s][:FQ]


def cin(embeddings, cot_first, cot_second, cot_third, w_first, w_second, w_third):
    samples, fields, width = embeddings.shape
    maps = cot_first.shape[1]
    e = jnp.pad(embeddings, ((0, 0), (0, FP - fields), (0, 0)))

    def columns(cot):
        cot = jnp.pad(cot.astype(F32), ((0, 0), (0, HP - maps)))
        return jnp.transpose(cot.reshape(samples // 2, 2, HP), (0, 2, 1))

    top = jnp.einsum("hij,nh->nij", w_third, cot_third, preferred_element_type=F32)
    top = jnp.pad(top, ((0, 0), (0, HP - maps), (0, FP - fields)))
    thi, tlo = halves(top)
    uhi, ulo = jnp.swapaxes(thi, 1, 2), jnp.swapaxes(tlo, 1, 2)

    w2b = jnp.pad(jnp.transpose(w_second, (2, 1, 0)), ((0, 0), (0, HP - maps), (0, KP - maps)))
    w2b = w2b.reshape(fields * HP, KP)
    w2f = w2b.T[:HP]
    w1t = jnp.pad(jnp.transpose(w_first, (2, 1, 0)), ((0, 0), (0, FP - fields), (0, HP - maps)))
    w1f = w1t.reshape(fields * FP, HP).T
    both = w_first.astype(F32)
    both = both + jnp.swapaxes(both, 1, 2)
    both = jnp.pad(jnp.transpose(both, (2, 1, 0)), ((0, FQ - fields), (0, FQ - fields), (0, KP - maps)))
    w1b = jnp.concatenate(halves(both), axis=2).reshape(FQ * FQ, 2 * KP)

    def per(*shape):
        return pl.BlockSpec(shape, lambda g: (g,) + (0,) * (len(shape) - 1))

    def whole(x):
        return pl.BlockSpec(x.shape, lambda g: (0,) * x.ndim, pipeline_mode=pl.Buffered(1))

    def kernel(*refs):
        cin_kernel(fields, *refs)

    return pl.pallas_call(
        kernel,
        grid=(samples // 2,),
        in_specs=[
            per(2, FP, width), per(1, HP, 2), per(1, HP, 2),
            per(2, HP, FP), per(2, HP, FP), per(2, FP, HP), per(2, FP, HP),
            whole(w1f), whole(w2f), whole(w2b), whole(w1b),
        ],
        out_specs=per(2, FQ, width),
        out_shape=jax.ShapeDtypeStruct((samples, FQ, width), F32),
        scratch_shapes=[
            pltpu.VMEM((FP, 256), F32),
            pltpu.VMEM((fields * FP, 256), BF),
            pltpu.VMEM((fields * HP, 256), BF),
            pltpu.VMEM((HP, 256), F32),
            pltpu.VMEM((2, JC * HP, 256), F32),
            pltpu.VMEM((2, 8 * FQ, 256), F32),
            pltpu.VMEM((FQ, 8, 256), F32),
            pltpu.VMEM((HP, 256), F32),
        ],
        compiler_params=pltpu.CompilerParams(vmem_limit_bytes=48 << 20),
        name="cin",
    )(e, columns(cot_first), columns(cot_second), thi, tlo, uhi, ulo, w1f, w2f, w2b, w1b)


def ranks(row_list, capacity, rows_dev):
    owner = row_list // rows_dev
    within = jnp.zeros_like(owner)
    for k in range(1, capacity):
        earlier = jnp.concatenate([jnp.full((k,), -1, jnp.int32), owner[:-k]])
        within = within + (earlier == owner).astype(jnp.int32)
    return owner, within, row_list - owner * rows_dev


def by_owner(owner, within, inside, owners, capacity):
    hot = (jnp.arange(owners, dtype=jnp.int32)[:, None] == owner[None, :]).astype(BF)
    places = jnp.arange(capacity, dtype=jnp.int32)[None, :]
    value = jnp.where(within[:, None] == places, inside[:, None] + 1, 0)
    value = jnp.concatenate([value // 64, value % 64], axis=1).astype(BF)
    found = jnp.dot(hot, value, preferred_element_type=F32)
    return (found[:, :capacity] * 64 + found[:, capacity:]).astype(jnp.int32) - 1


def merge_kernel(inv_ref, target_ref, grads_ref, out_ref, hot, pair):
    count, listed = pair.shape[0], target_ref.shape[1]
    pair[...] = jnp.concatenate(halves(grads_ref[...]), axis=1)
    merged = []
    rows = 256
    for b in range(listed // rows):
        place = lax.broadcasted_iota(jnp.int32, (rows, count), 0) + b * rows
        hot[...] = jnp.where(place == inv_ref[...], 1.0, 0.0).astype(BF)
        m = dot(hot[...], pair[...])
        merged.append(m[:, :128] + m[:, 128:])
    merged = jnp.concatenate(halves(jnp.concatenate(merged, axis=0)), axis=1)
    for b in range(out_ref.shape[0] // rows):
        place = lax.broadcasted_iota(jnp.int32, (rows, listed), 0) + b * rows
        m = dot(jnp.where(place == target_ref[...], 1.0, 0.0).astype(BF), merged)
        out_ref[b * rows : (b + 1) * rows, :] = m[:, :128] + m[:, 128:]


def merge(grads, inverse, target, slots):
    samples, padded, width = grads.shape
    inv = jnp.pad(inverse, ((0, 0), (0, padded - inverse.shape[1])), constant_values=-1).reshape(1, -1)
    count = samples * padded
    return pl.pallas_call(
        merge_kernel,
        out_shape=jax.ShapeDtypeStruct((slots, width), F32),
        scratch_shapes=[pltpu.VMEM((256, count), BF), pltpu.VMEM((count, 2 * width), BF)],
        compiler_params=pltpu.CompilerParams(vmem_limit_bytes=32 << 20),
        name="merge",
    )(inv, target.reshape(1, -1), grads.reshape(count, width))


def update_kernel(loc_ref, rows_ref, table_ref, accum_ref, ask_ref, nt_ref, na_ref, found_ref, hot, pair, grad):
    pair[...] = jnp.concatenate(halves(rows_ref[...]), axis=1)
    got = pair.shape[0]
    lane = lax.broadcasted_iota(jnp.int32, (128, 128), 1)
    for b in range(table_ref.shape[0] // 1024):
        for r in range(8):
            place = lax.broadcasted_iota(jnp.int32, (128, got), 0) + (b * 1024 + r * 128)
            hot[r * 128 : (r + 1) * 128, :] = jnp.where(place == loc_ref[...], 1.0, 0.0).astype(BF)
        g = dot(hot[...], pair[...])
        grad[...] = g[:, :128] + g[:, 128:]
        means = jnp.zeros((128, 128), F32)
        for r in range(8):
            part = grad[r * 128 : (r + 1) * 128, :]
            means = jnp.where(lane == r, jnp.mean(part * part, axis=1, keepdims=True), means)
        na = accum_ref[8 * b : 8 * b + 8, :] + means.T[:8]
        na_ref[8 * b : 8 * b + 8, :] = na
        scale = RATE / (jnp.sqrt(na) + EPS)
        scale = jnp.concatenate([scale, jnp.zeros((120, 128), F32)], axis=0).T
        for r in range(8):
            at = slice(b * 1024 + r * 128, b * 1024 + (r + 1) * 128)
            nt_ref[at, :] = table_ref[at, :] - grad[r * 128 : (r + 1) * 128, :] * scale[:, r : r + 1]

    def gather(k, carry):
        for t in range(8):
            found_ref[pl.ds(k * 8 + t, 1), :] = nt_ref[pl.ds(ask_ref[k * 8 + t], 1), :]
        return carry

    lax.fori_loop(0, found_ref.shape[0] // 8, gather, 0)


def update(locs, rows, table, accum, asks):
    rows_dev, width = table.shape
    vmem = pl.BlockSpec(memory_space=pltpu.VMEM)
    new_table, new_accum, found = pl.pallas_call(
        update_kernel,
        in_specs=[vmem, vmem, vmem, vmem, pl.BlockSpec(memory_space=pltpu.SMEM)],
        out_specs=[vmem, vmem, vmem],
        out_shape=[
            jax.ShapeDtypeStruct(table.shape, F32),
            jax.ShapeDtypeStruct((rows_dev // 128, 128), F32),
            jax.ShapeDtypeStruct((asks.shape[0], width), F32),
        ],
        scratch_shapes=[
            pltpu.VMEM((1024, rows.shape[0]), BF),
            pltpu.VMEM((rows.shape[0], 2 * width), BF),
            pltpu.VMEM((1024, width), F32),
        ],
        compiler_params=pltpu.CompilerParams(vmem_limit_bytes=48 << 20),
        name="update",
    )(locs.reshape(1, -1), rows, table, accum.reshape(rows_dev // 128, 128), asks)
    return new_table, new_accum.reshape(rows_dev), found


def pick_kernel(index_ref, rows_ref, out_ref):
    def gather(k, carry):
        for t in range(8):
            out_ref[pl.ds(k * 8 + t, 1), :] = rows_ref[pl.ds(index_ref[k * 8 + t], 1), :]
        return carry

    lax.fori_loop(0, out_ref.shape[0] // 8, gather, 0)


def pick(rows, index):
    vmem = pl.BlockSpec(memory_space=pltpu.VMEM)
    return pl.pallas_call(
        pick_kernel,
        in_specs=[pl.BlockSpec(memory_space=pltpu.SMEM), vmem],
        out_specs=vmem,
        out_shape=jax.ShapeDtypeStruct((index.shape[0], rows.shape[1]), F32),
        compiler_params=pltpu.CompilerParams(vmem_limit_bytes=32 << 20),
        name="pick",
    )(index, rows)


def exchange(parts):
    return lax.all_to_all(parts, ("group", "member"), split_axis=0, concat_axis=0, tiled=True)


def local(
    embeddings,
    cot_first,
    cot_second,
    cot_third,
    w_first,
    w_second,
    w_third,
    unique_ids,
    inverse,
    table,
    accum,
    next_ids,
):
    rows_dev, width = table.shape
    owners = lax.axis_size("group") * lax.axis_size("member")
    owner, within, inside = ranks(unique_ids[0], CAP, rows_dev)
    target = owner * CAP + within
    ask_owner, ask_within, ask_inside = ranks(next_ids[0], RCAP, rows_dev)
    ask_target = ask_owner * RCAP + ask_within
    numbers = jnp.concatenate(
        [
            by_owner(owner, within, inside, owners, CAP),
            by_owner(ask_owner, ask_within, ask_inside, owners, RCAP),
        ],
        axis=1,
    )
    numbers = exchange(numbers)
    locs = numbers[:, :CAP].reshape(-1)
    asks = jnp.maximum(numbers[:, CAP:], 0).reshape(-1)

    grads = cin(embeddings, cot_first, cot_second, cot_third, w_first, w_second, w_third)
    send = merge(grads, inverse, target, owners * CAP)
    rows = exchange(send.reshape(owners, CAP, width)).reshape(-1, width)
    new_table, new_accum, found = update(locs, rows, table, accum, asks)
    answers = exchange(found.reshape(owners, RCAP, width)).reshape(-1, width)
    return (new_table, new_accum, pick(answers, ask_target)[None])


def solution(mesh):
    in_specs = (
        P(("group", "member"), None, None),
        P(("group", "member"), None),
        P(("group", "member"), None),
        P(("group", "member"), None),
        P(),
        P(),
        P(),
        P(("group", "member"), None),
        P(("group", "member"), None),
        P(("group", "member"), None),
        P(("group", "member")),
        P(("group", "member"), None),
    )
    out_specs = (
        P(("group", "member"), None),
        P(("group", "member")),
        P(("group", "member"), None, None),
    )
    return jax.shard_map(local, mesh=mesh, in_specs=in_specs, out_specs=out_specs, check_vma=False)
```

```python
import jax
import jax.numpy as jnp
from jax import lax
from jax.experimental import pallas as pl
from jax.experimental.pallas import tpu as pltpu
from jax.sharding import PartitionSpec as P

CAP = 4
RCAP = 8
RATE = 0.5
EPS = 1e-08

BF = jnp.bfloat16
F32 = jnp.float32


def halves(x):
    hi = x.astype(BF)
    return hi, (x - hi.astype(F32)).astype(BF)


def dot(a, b):
    return jnp.dot(a, b, preferred_element_type=F32)


FP = 48
FQ = 40
HP = 112
HQ = 104
KP = 128
JC = 3


def cin_kernel(
    fields,
    e_ref, c1_ref, c2_ref, top_ref,
    w1f_ref, w2f_ref, w2b_ref, w1b_ref,
    out_ref,
    ef, p1, p2, l1f, mid, bot, part, l2s,
):
    lanes = 256
    e = jnp.concatenate([e_ref[0], e_ref[1]], axis=1)
    ef[...] = e.astype(F32)
    e3 = e.reshape(FP // 16, 16, lanes)

    def row16(i):
        return jnp.broadcast_to(ef[i : i + 1, :], (16, lanes)).astype(BF)

    uppers = []
    for s in range(2):
        hi, lo = halves(top_ref[s])
        rest = (top_ref[s] - hi.astype(F32) - lo.astype(F32)).astype(BF)
        grad_two = dot(hi, e_ref[s]) + (dot(lo, e_ref[s]) + dot(rest, e_ref[s]))
        uppers.append((c2_ref[0, :, s : s + 1] + grad_two).astype(BF))
    upper = jnp.concatenate(uppers, axis=1)
    upper = jnp.concatenate([upper, jnp.zeros((KP - HP, lanes), BF)], axis=0)

    for i in range(fields):
        p1[i * FP : (i + 1) * FP, :] = (e3 * row16(i)[None]).reshape(FP, lanes)
    l1 = dot(w1f_ref[...], p1[...]).astype(BF)
    l1f[...] = l1.astype(F32)
    l3 = l1.reshape(HP // 16, 16, lanes)

    acc = [jnp.zeros((HQ // 8, 8, 128), F32) for _ in range(2)]
    done = 0
    l2 = None
    for c in range(fields // JC):
        mid[c % 2] = dot(w2b_ref[c * JC * HP : (c + 1) * JC * HP, :], upper)
        for k in range(JC):
            j = c * JC + k
            p2[j * HP : (j + 1) * HP, :] = (l3 * row16(j)[None]).reshape(HP, lanes)
        ready = (c + 1) * JC * HP
        if c + 1 < fields // JC:
            ready = ready // 512 * 512
        if ready > done:
            piece = dot(w2f_ref[:, done:ready], p2[done:ready, :])
            if done:
                piece = piece + l2s[...]
            l2s[...] = piece
            done = ready
        for s in range(2):
            ls = slice(s * 128, (s + 1) * 128)
            one = l1f[:HQ, ls].reshape(HQ // 8, 8, 128)
            for k in range(JC):
                j = c * JC + k
                m = mid[c % 2, k * HP : k * HP + HQ, ls].reshape(HQ // 8, 8, 128)
                b = jnp.broadcast_to(ef[j : j + 1, ls], (8, 128))
                acc[s] = acc[s] + m * b[None]
                part[j, :, ls] = jnp.sum(m * one, axis=0)
    l2 = l2s[...].astype(BF)
    bases = []
    for s in range(2):
        hi, lo = halves(top_ref[s].T)
        both = l2[:, s * 128 : (s + 1) * 128]
        bases.append(dot(hi, both) + dot(lo, both))
    lower = jnp.concatenate(
        [(c1_ref[0, :HQ, s : s + 1] + acc[s].reshape(HQ, 128)).astype(F32) for s in range(2)], axis=1
    )
    lower = jnp.concatenate([lower, jnp.zeros((KP - HQ, lanes), F32)], axis=0).astype(BF)
    lower = jnp.concatenate([lower, lower], axis=0)
    for c in range(FQ // 8):
        buf = c % 2
        bot[buf] = dot(w1b_ref[c * 8 * FQ : (c + 1) * 8 * FQ, :], lower)
        for s in range(2):
            ls = slice(s * 128, (s + 1) * 128)
            es = ef[:FQ, ls].reshape(FQ // 8, 8, 128)
            for k in range(8):
                j = c * 8 + k
                m = bot[buf, k * FQ : (k + 1) * FQ, ls].reshape(FQ // 8, 8, 128)
                t = jnp.sum(m * es, axis=0)
                if j < fields:
                    t = t + part[j, :, ls]
                part[j, :, ls] = t
    for s in range(2):
        ls = slice(s * 128, (s + 1) * 128)
        out_ref[s] = jnp.sum(part[:, :, ls], axis=1) + bases[s][:FQ]


def cin(embeddings, cot_first, cot_second, cot_third, w_first, w_second, w_third):
    samples, fields, width = embeddings.shape
    maps = cot_first.shape[1]
    e = jnp.pad(embeddings, ((0, 0), (0, FP - fields), (0, 0)))

    def columns(cot):
        cot = jnp.pad(cot.astype(F32), ((0, 0), (0, HP - maps)))
        return jnp.transpose(cot.reshape(samples // 2, 2, HP), (0, 2, 1))

    w_third = jnp.pad(w_third, ((0, 0), (0, HP - maps), (0, FP - fields)))
    top = jnp.einsum("hij,nh->nij", w_third, cot_third, preferred_element_type=F32)

    w2b = jnp.pad(jnp.transpose(w_second, (2, 1, 0)), ((0, 0), (0, HP - maps), (0, KP - maps)))
    w2b = w2b.reshape(fields * HP, KP)
    w2f = w2b.T[:HP]
    w1t = jnp.pad(jnp.transpose(w_first, (2, 1, 0)), ((0, 0), (0, FP - fields), (0, HP - maps)))
    w1f = w1t.reshape(fields * FP, HP).T
    both = w_first.astype(F32)
    both = both + jnp.swapaxes(both, 1, 2)
    both = jnp.pad(jnp.transpose(both, (2, 1, 0)), ((0, FQ - fields), (0, FQ - fields), (0, KP - maps)))
    w1b = jnp.concatenate(halves(both), axis=2).reshape(FQ * FQ, 2 * KP)

    def per(*shape):
        return pl.BlockSpec(shape, lambda g: (g,) + (0,) * (len(shape) - 1))

    def whole(x):
        return pl.BlockSpec(x.shape, lambda g: (0,) * x.ndim, pipeline_mode=pl.Buffered(1))

    def kernel(*refs):
        cin_kernel(fields, *refs)

    return pl.pallas_call(
        kernel,
        grid=(samples // 2,),
        in_specs=[
            per(2, FP, width), per(1, HP, 2), per(1, HP, 2),
            per(2, HP, FP),
            whole(w1f), whole(w2f), whole(w2b), whole(w1b),
        ],
        out_specs=per(2, FQ, width),
        out_shape=jax.ShapeDtypeStruct((samples, FQ, width), F32),
        scratch_shapes=[
            pltpu.VMEM((FP, 256), F32),
            pltpu.VMEM((fields * FP, 256), BF),
            pltpu.VMEM((fields * HP, 256), BF),
            pltpu.VMEM((HP, 256), F32),
            pltpu.VMEM((2, JC * HP, 256), F32),
            pltpu.VMEM((2, 8 * FQ, 256), F32),
            pltpu.VMEM((FQ, 8, 256), F32),
            pltpu.VMEM((HP, 256), F32),
        ],
        compiler_params=pltpu.CompilerParams(vmem_limit_bytes=48 << 20),
        name="cin",
    )(e, columns(cot_first), columns(cot_second), top, w1f, w2f, w2b, w1b)


def ranks(row_list, capacity, rows_dev):
    owner = row_list // rows_dev
    within = jnp.zeros_like(owner)
    for k in range(1, capacity):
        earlier = jnp.concatenate([jnp.full((k,), -1, jnp.int32), owner[:-k]])
        within = within + (earlier == owner).astype(jnp.int32)
    return owner, within, row_list - owner * rows_dev


def by_owner(owner, within, inside, owners, capacity):
    hot = (jnp.arange(owners, dtype=jnp.int32)[:, None] == owner[None, :]).astype(BF)
    places = jnp.arange(capacity, dtype=jnp.int32)[None, :]
    value = jnp.where(within[:, None] == places, inside[:, None] + 1, 0)
    value = jnp.concatenate([value // 64, value % 64], axis=1).astype(BF)
    found = jnp.dot(hot, value, preferred_element_type=F32)
    return (found[:, :capacity] * 64 + found[:, capacity:]).astype(jnp.int32) - 1


MESH = pl.DeviceIdType.MESH
COPIES = 77


def moved(step):
    group, member = lax.axis_index("group"), lax.axis_index("member")
    x, z, core = member // 16, (member // 2) % 8, member % 2
    x = (x + (step // 16) % 4) % 4
    z = (z + (step // 2) % 8) % 8
    return (group + step // 64) % 4, x * 16 + z * 2 + (core + step % 2) % 2


class Tree:
    def __init__(self):
        self.sem = pltpu.get_barrier_semaphore()
        self.group, member = lax.axis_index("group"), lax.axis_index("member")
        self.x, self.rest = member // 16, member % 16
        top = self.group * 4 + self.x
        self.root = jnp.logical_and(top == 0, self.rest == 0)
        self.leader = jnp.logical_and(top != 0, self.rest == 0)

    def signal(self, group, member):
        pl.semaphore_signal(self.sem, inc=1, device_id=(group, member), device_id_type=MESH)

    def arrive(self):
        @pl.when(self.rest != 0)
        def _():
            self.signal(self.group, self.x * 16)

    def pass_up(self):
        @pl.when(self.leader)
        def _():
            pl.semaphore_wait(self.sem, 15)
            self.signal(0, 0)

    def turn(self):
        @pl.when(self.root)
        def _():
            pl.semaphore_wait(self.sem, 30)

            def tell(k, carry):
                self.signal(k // 4, (k % 4) * 16)
                return carry

            lax.fori_loop(1, 16, tell, 0)

    def release(self):
        @pl.when(jnp.logical_not(self.root))
        def _():
            pl.semaphore_wait(self.sem, 1)

        @pl.when(self.rest == 0)
        def _():
            def tell(k, carry):
                self.signal(self.group, self.x * 16 + k)
                return carry

            lax.fori_loop(1, 16, tell, 0)


def step_kernel(
    inv_ref, target_ref, grads_ref, numbers_ref, table_ref, accum_ref,
    nt_ref, na_ref, answers_ref,
    hot, pair, grad, send, rows, found, ask_v, ask_s, rows_out, rows_in, answers_out, answers_in, own,
):
    tree = Tree()
    tree.arrive()
    owners, width = numbers_ref.shape
    me = lax.axis_index("group") * 64 + lax.axis_index("member")
    count, listed = inv_ref.shape[1], target_ref.shape[1]

    g = jnp.concatenate(halves(grads_ref[...]), axis=1)
    merged = []
    for b in range(listed // 256):
        place = lax.broadcasted_iota(jnp.int32, (256, count), 0) + b * 256
        m = dot(jnp.where(place == inv_ref[...], 1.0, 0.0).astype(BF), g)
        merged.append(m[:, :width] + m[:, width:])
    merged = jnp.concatenate(halves(jnp.concatenate(merged, axis=0)), axis=1)
    tree.pass_up()
    for c in range(CAP):
        place = lax.broadcasted_iota(jnp.int32, (owners, listed), 0) + c * owners
        m = dot(jnp.where(place == target_ref[...], 1.0, 0.0).astype(BF), merged)
        send[:, c, :] = m[:, :width] + m[:, width:]
    send[:, CAP, :] = numbers_ref[...]
    tree.turn()
    rows[me] = send[me]
    tree.release()

    def send_rows(k, carry):
        group, member = moved((k * COPIES) % owners)
        pltpu.make_async_remote_copy(
            src_ref=send.at[group * 64 + member], dst_ref=rows.at[me],
            send_sem=rows_out, recv_sem=rows_in,
            device_id=(group, member), device_id_type=MESH,
        ).start()
        return carry

    lax.fori_loop(1, owners, send_rows, 0)
    others = pl.ds(0, owners - 1)
    pltpu.make_async_copy(send.at[others], rows.at[others], rows_in).wait()

    numbers = rows[:, CAP, :].T[:16].astype(jnp.int32)
    ask_v[...] = jnp.clip(numbers, 0, table_ref.shape[0] - 1)
    to_scalars = pltpu.make_async_copy(ask_v, ask_s, own)
    to_scalars.start()
    for c in range(CAP):
        pair[c * owners : (c + 1) * owners, :] = jnp.concatenate(halves(rows[:, c, :]), axis=1)
    lane = lax.broadcasted_iota(jnp.int32, (128, 128), 1)
    for b in range(table_ref.shape[0] // 1024):
        for r in range(8):
            place = lax.broadcasted_iota(jnp.int32, (128, owners), 0) + (b * 1024 + r * 128)
            for c in range(CAP):
                hit = place == numbers[c : c + 1, :]
                hot[r * 128 : (r + 1) * 128, c * owners : (c + 1) * owners] = jnp.where(hit, 1.0, 0.0).astype(BF)
        s = dot(hot[...], pair[...])
        grad[...] = s[:, :width] + s[:, width:]
        means = jnp.zeros((128, 128), F32)
        for r in range(8):
            part = grad[r * 128 : (r + 1) * 128, :]
            means = jnp.where(lane == r, jnp.mean(part * part, axis=1, keepdims=True), means)
        na = accum_ref[8 * b : 8 * b + 8, :] + means.T[:8]
        na_ref[8 * b : 8 * b + 8, :] = na
        scale = RATE / (jnp.sqrt(na) + EPS)
        scale = jnp.concatenate([scale, jnp.zeros((120, 128), F32)], axis=0).T
        for r in range(8):
            at = slice(b * 1024 + r * 128, b * 1024 + (r + 1) * 128)
            nt_ref[at, :] = table_ref[at, :] - grad[r * 128 : (r + 1) * 128, :] * scale[:, r : r + 1]
    to_scalars.wait()

    def look_up(p, out):
        for t in range(RCAP):
            row = jnp.clip(ask_s[CAP + t, p], 0, nt_ref.shape[0] - 1)
            out[p, t : t + 1, :] = nt_ref[pl.ds(row, 1), :]

    late = 4

    def gather(k):
        group, member = moved((k * COPIES) % owners)
        look_up(group * 64 + member, found)

    def send_answers(k):
        group, member = moved((k * COPIES) % owners)
        pltpu.make_async_remote_copy(
            src_ref=found.at[group * 64 + member], dst_ref=answers_ref.at[me],
            send_sem=answers_out, recv_sem=answers_in,
            device_id=(group, member), device_id_type=MESH,
        ).start()

    def first(k, carry):
        gather(k)
        return carry

    def both(k, carry):
        gather(k)
        send_answers(k - late)
        return carry

    def last(k, carry):
        send_answers(k)
        return carry

    lax.fori_loop(1, 1 + late, first, 0)
    lax.fori_loop(1 + late, owners, both, 0)
    look_up(me, answers_ref)
    lax.fori_loop(owners - late, owners, last, 0)
    pltpu.make_async_copy(send.at[others], rows.at[others], rows_out).wait()
    pltpu.make_async_copy(found.at[others], answers_ref.at[others], answers_in).wait()
    pltpu.make_async_copy(found.at[others], answers_ref.at[others], answers_out).wait()


def step(grads, inverse, target, numbers, table, accum):
    samples, padded, width = grads.shape
    owners = numbers.shape[0]
    rows_dev = table.shape[0]
    inv = jnp.pad(inverse, ((0, 0), (0, padded - inverse.shape[1])), constant_values=-1).reshape(1, -1)
    vmem = pl.BlockSpec(memory_space=pltpu.VMEM)
    new_table, new_accum, answers = pl.pallas_call(
        step_kernel,
        in_specs=[vmem] * 6,
        out_specs=[vmem] * 3,
        out_shape=[
            jax.ShapeDtypeStruct(table.shape, F32),
            jax.ShapeDtypeStruct((rows_dev // 128, 128), F32),
            jax.ShapeDtypeStruct((owners, RCAP, width), F32),
        ],
        scratch_shapes=[
            pltpu.VMEM((1024, CAP * owners), BF),
            pltpu.VMEM((CAP * owners, 2 * width), BF),
            pltpu.VMEM((1024, width), F32),
            pltpu.VMEM((owners, CAP + 1, width), F32),
            pltpu.VMEM((owners, CAP + 1, width), F32),
            pltpu.VMEM((owners, RCAP, width), F32),
            pltpu.VMEM((16, owners), jnp.int32),
            pltpu.SMEM((16, owners), jnp.int32),
            pltpu.SemaphoreType.DMA,
            pltpu.SemaphoreType.DMA,
            pltpu.SemaphoreType.DMA,
            pltpu.SemaphoreType.DMA,
            pltpu.SemaphoreType.DMA,
        ],
        compiler_params=pltpu.CompilerParams(
            collective_id=0, has_side_effects=True, vmem_limit_bytes=56 << 20
        ),
        name="step",
    )(inv, target.reshape(1, -1), grads.reshape(samples * padded, width), numbers, table,
      accum.reshape(rows_dev // 128, 128))
    return new_table, new_accum.reshape(rows_dev), answers


def pick_kernel(index_ref, rows_ref, out_ref):
    def gather(k, carry):
        for t in range(8):
            out_ref[pl.ds(k * 8 + t, 1), :] = rows_ref[pl.ds(index_ref[k * 8 + t], 1), :]
        return carry

    lax.fori_loop(0, out_ref.shape[0] // 8, gather, 0)


def pick(rows, index):
    vmem = pl.BlockSpec(memory_space=pltpu.VMEM)
    return pl.pallas_call(
        pick_kernel,
        in_specs=[pl.BlockSpec(memory_space=pltpu.SMEM), vmem],
        out_specs=vmem,
        out_shape=jax.ShapeDtypeStruct((index.shape[0], rows.shape[1]), F32),
        compiler_params=pltpu.CompilerParams(vmem_limit_bytes=32 << 20),
        name="pick",
    )(index, rows)


def local(
    embeddings,
    cot_first,
    cot_second,
    cot_third,
    w_first,
    w_second,
    w_third,
    unique_ids,
    inverse,
    table,
    accum,
    next_ids,
):
    rows_dev, width = table.shape
    owners = lax.axis_size("group") * lax.axis_size("member")
    owner, within, inside = ranks(unique_ids[0], CAP, rows_dev)
    target = within * owners + owner
    ask_owner, ask_within, ask_inside = ranks(next_ids[0], RCAP, rows_dev)
    ask_target = ask_owner * RCAP + ask_within
    numbers = jnp.concatenate(
        [
            by_owner(owner, within, inside, owners, CAP),
            by_owner(ask_owner, ask_within, ask_inside, owners, RCAP),
        ],
        axis=1,
    )
    numbers = jnp.pad(numbers.astype(F32), ((0, 0), (0, width - CAP - RCAP)))
    grads = cin(embeddings, cot_first, cot_second, cot_third, w_first, w_second, w_third)
    new_table, new_accum, answers = step(grads, inverse, target, numbers, table, accum)
    return (new_table, new_accum, pick(answers.reshape(-1, width), ask_target)[None])


def solution(mesh):
    in_specs = (
        P(("group", "member"), None, None),
        P(("group", "member"), None),
        P(("group", "member"), None),
        P(("group", "member"), None),
        P(),
        P(),
        P(),
        P(("group", "member"), None),
        P(("group", "member"), None),
        P(("group", "member"), None),
        P(("group", "member")),
        P(("group", "member"), None),
    )
    out_specs = (
        P(("group", "member"), None),
        P(("group", "member")),
        P(("group", "member"), None, None),
    )
    return jax.shard_map(local, mesh=mesh, in_specs=in_specs, out_specs=out_specs, check_vma=False)
```

```python
import jax
import jax.numpy as jnp
from jax import lax
from jax.experimental import pallas as pl
from jax.experimental.pallas import tpu as pltpu
from jax.sharding import PartitionSpec as P

FIELDS = 39
CAP = 4
RCAP = 8
RATE = 0.5
EPS = 1e-08

BF = jnp.bfloat16
F32 = jnp.float32


def halves(x):
    hi = x.astype(BF)
    return hi, (x - hi.astype(F32)).astype(BF)


def dot(a, b):
    return jnp.dot(a, b, preferred_element_type=F32)


FP = 48
FQ = 40
HP = 112
HQ = 104
KP = 128
JC = 3


def cin_pair(
    fields, g,
    e_ref, c1_ref, c2_ref, top_ref, w1f_ref, w2f_ref, w2b_ref, w1b_ref,
    out_ref,
    ef, p1, p2, l1f, mid, bot, part, l2s,
):
    lanes = 256
    c1, c2 = c1_ref[g], c2_ref[g]
    e = jnp.concatenate([e_ref[2 * g], e_ref[2 * g + 1]], axis=1)
    ef[...] = e.astype(F32)
    e3 = e.reshape(FP // 16, 16, lanes)

    def row16(i):
        return jnp.broadcast_to(ef[i : i + 1, :], (16, lanes)).astype(BF)

    uppers = []
    for s in range(2):
        top, one = top_ref[2 * g + s], e[:, s * 128 : (s + 1) * 128]
        hi, lo = halves(top)
        rest = (top - hi.astype(F32) - lo.astype(F32)).astype(BF)
        grad_two = dot(hi, one) + (dot(lo, one) + dot(rest, one))
        uppers.append((c2[:, s : s + 1] + grad_two).astype(BF))
    upper = jnp.concatenate(uppers, axis=1)
    upper = jnp.concatenate([upper, jnp.zeros((KP - HP, lanes), BF)], axis=0)

    for i in range(fields):
        p1[i * FP : (i + 1) * FP, :] = (e3 * row16(i)[None]).reshape(FP, lanes)
    l1 = dot(w1f_ref[...], p1[...]).astype(BF)
    l1f[...] = l1.astype(F32)
    l3 = l1.reshape(HP // 16, 16, lanes)

    acc = [jnp.zeros((HQ // 8, 8, 128), F32) for _ in range(2)]
    done = 0
    l2 = None
    for c in range(fields // JC):
        mid[c % 2] = dot(w2b_ref[c * JC * HP : (c + 1) * JC * HP, :], upper)
        for k in range(JC):
            j = c * JC + k
            p2[j * HP : (j + 1) * HP, :] = (l3 * row16(j)[None]).reshape(HP, lanes)
        ready = (c + 1) * JC * HP
        if c + 1 < fields // JC:
            ready = ready // 512 * 512
        if ready > done:
            piece = dot(w2f_ref[:, done:ready], p2[done:ready, :])
            if done:
                piece = piece + l2s[...]
            l2s[...] = piece
            done = ready
        for s in range(2):
            ls = slice(s * 128, (s + 1) * 128)
            one = l1f[:HQ, ls].reshape(HQ // 8, 8, 128)
            for k in range(JC):
                j = c * JC + k
                m = mid[c % 2, k * HP : k * HP + HQ, ls].reshape(HQ // 8, 8, 128)
                b = jnp.broadcast_to(ef[j : j + 1, ls], (8, 128))
                acc[s] = acc[s] + m * b[None]
                part[j, :, ls] = jnp.sum(m * one, axis=0)
    l2 = l2s[...].astype(BF)
    bases = []
    for s in range(2):
        hi, lo = halves(top_ref[2 * g + s].T)
        both = l2[:, s * 128 : (s + 1) * 128]
        bases.append(dot(hi, both) + dot(lo, both))
    lower = jnp.concatenate(
        [(c1[:HQ, s : s + 1] + acc[s].reshape(HQ, 128)).astype(F32) for s in range(2)], axis=1
    )
    lower = jnp.concatenate([lower, jnp.zeros((KP - HQ, lanes), F32)], axis=0).astype(BF)
    lower = jnp.concatenate([lower, lower], axis=0)
    for c in range(FQ // 8):
        buf = c % 2
        bot[buf] = dot(w1b_ref[c * 8 * FQ : (c + 1) * 8 * FQ, :], lower)
        for s in range(2):
            ls = slice(s * 128, (s + 1) * 128)
            es = ef[:FQ, ls].reshape(FQ // 8, 8, 128)
            for k in range(8):
                j = c * 8 + k
                m = bot[buf, k * FQ : (k + 1) * FQ, ls].reshape(FQ // 8, 8, 128)
                t = jnp.sum(m * es, axis=0)
                if j < fields:
                    t = t + part[j, :, ls]
                part[j, :, ls] = t
    for s in range(2):
        ls = slice(s * 128, (s + 1) * 128)
        out_ref[2 * g + s] = jnp.sum(part[:, :, ls], axis=1) + bases[s][:FQ]


def cin_operands(embeddings, cot_first, cot_second, cot_third, w_first, w_second, w_third):
    samples, fields, width = embeddings.shape
    maps = cot_first.shape[1]
    e = jnp.pad(embeddings, ((0, 0), (0, FP - fields), (0, 0)))

    def columns(cot):
        cot = jnp.pad(cot.astype(F32), ((0, 0), (0, HP - maps)))
        return jnp.transpose(cot.reshape(samples // 2, 2, HP), (0, 2, 1))

    w_third = jnp.pad(w_third, ((0, 0), (0, HP - maps), (0, FP - fields)))
    top = jnp.einsum("hij,nh->nij", w_third, cot_third, preferred_element_type=F32)

    w2b = jnp.pad(jnp.transpose(w_second, (2, 1, 0)), ((0, 0), (0, HP - maps), (0, KP - maps)))
    w2b = w2b.reshape(fields * HP, KP)
    w2f = w2b.T[:HP]
    w1t = jnp.pad(jnp.transpose(w_first, (2, 1, 0)), ((0, 0), (0, FP - fields), (0, HP - maps)))
    w1f = w1t.reshape(fields * FP, HP).T
    both = w_first.astype(F32)
    both = both + jnp.swapaxes(both, 1, 2)
    both = jnp.pad(jnp.transpose(both, (2, 1, 0)), ((0, FQ - fields), (0, FQ - fields), (0, KP - maps)))
    w1b = jnp.concatenate(halves(both), axis=2).reshape(FQ * FQ, 2 * KP)
    return e, columns(cot_first), columns(cot_second), top, w1f, w2f, w2b, w1b


def cin_scratch(fields):
    return [
        pltpu.VMEM((FP, 256), F32),
        pltpu.VMEM((fields * FP, 256), BF),
        pltpu.VMEM((fields * HP, 256), BF),
        pltpu.VMEM((HP, 256), F32),
        pltpu.VMEM((2, JC * HP, 256), F32),
        pltpu.VMEM((2, 8 * FQ, 256), F32),
        pltpu.VMEM((FQ, 8, 256), F32),
        pltpu.VMEM((HP, 256), F32),
    ]


def ranks(row_list, capacity, rows_dev):
    owner = row_list // rows_dev
    lane = lax.broadcasted_iota(jnp.int32, owner.shape, 1)
    within = jnp.zeros_like(owner)
    for k in range(1, capacity):
        same = jnp.logical_and(pltpu.roll(owner, k, 1) == owner, lane >= k)
        within = within + jnp.where(same, 1, 0)
    return owner, within, row_list - owner * rows_dev


def by_owner(owner, within, inside, owners, capacity):
    hot = lax.broadcasted_iota(jnp.int32, (owners, owner.shape[1]), 0) == owner
    hot = jnp.where(hot, 1.0, 0.0).astype(BF)
    place = lax.broadcasted_iota(jnp.int32, (8, owner.shape[1]), 0)
    value = jnp.where(place == within, inside + 1, 0)
    high = value // 64
    value = jnp.concatenate([high.astype(F32), (value - high * 64).astype(F32)], axis=0).astype(BF)
    found = lax.dot_general(hot, value, (((1,), (1,)), ((), ())), preferred_element_type=F32)
    return found[:, :8] * 64 + found[:, 8:] - 1


MESH = pl.DeviceIdType.MESH
COPIES = 77


def moved(step):
    group, member = lax.axis_index("group"), lax.axis_index("member")
    x, z, core = member // 16, (member // 2) % 8, member % 2
    x = (x + (step // 16) % 4) % 4
    z = (z + (step // 2) % 8) % 8
    return (group + step // 64) % 4, x * 16 + z * 2 + (core + step % 2) % 2


class Tree:
    def __init__(self):
        self.sem = pltpu.get_barrier_semaphore()
        self.group, member = lax.axis_index("group"), lax.axis_index("member")
        self.x, self.rest = member // 16, member % 16
        top = self.group * 4 + self.x
        self.root = jnp.logical_and(top == 0, self.rest == 0)
        self.leader = jnp.logical_and(top != 0, self.rest == 0)

    def signal(self, group, member):
        pl.semaphore_signal(self.sem, inc=1, device_id=(group, member), device_id_type=MESH)

    def arrive(self):
        @pl.when(self.rest != 0)
        def _():
            self.signal(self.group, self.x * 16)

    def pass_up(self):
        @pl.when(self.leader)
        def _():
            pl.semaphore_wait(self.sem, 15)
            self.signal(0, 0)

    def turn(self):
        @pl.when(self.root)
        def _():
            pl.semaphore_wait(self.sem, 30)

            def tell(k, carry):
                self.signal(k // 4, (k % 4) * 16)
                return carry

            lax.fori_loop(1, 16, tell, 0)

    def release(self):
        @pl.when(jnp.logical_not(self.root))
        def _():
            pl.semaphore_wait(self.sem, 1)

        @pl.when(self.rest == 0)
        def _():
            def tell(k, carry):
                self.signal(self.group, self.x * 16 + k)
                return carry

            lax.fori_loop(1, 16, tell, 0)


def step_kernel(
    inv_ref, ids_ref, next_ref, table_ref, accum_ref,
    e_ref, c1_ref, c2_ref, top_ref, w1f_ref, w2f_ref, w2b_ref, w1b_ref,
    nt_out, na_ref, answers_ref,
    nt_ref, hot, pair, grad, grads, send, rows, found, ask_v, ask_s, rows_out, rows_in, answers_out, answers_in, own, table_in, table_out,
    *scratch,
):
    tree = Tree()
    tree.arrive()
    table_copy = pltpu.make_async_copy(table_ref, nt_ref, table_in)
    table_copy.start()
    owners, width = send.shape[0], send.shape[2]
    rows_dev = table_ref.shape[0]
    me = lax.axis_index("group") * 64 + lax.axis_index("member")
    count, listed = inv_ref.shape[1], ids_ref.shape[1]

    owner, within, inside = ranks(ids_ref[...], CAP, rows_dev)
    target = within * owners + owner
    ask_owner, ask_within, ask_inside = ranks(next_ref[...], RCAP, rows_dev)
    numbers = [
        by_owner(owner, within, inside, owners, CAP),
        by_owner(ask_owner, ask_within, ask_inside, owners, RCAP),
    ]
    send[:, CAP, :] = jnp.concatenate(numbers + [jnp.zeros((owners, width - 16), F32)], axis=1)

    steps = e_ref.shape[0] // 2

    def cin_step(g, carry):
        pl.when(g == steps // 4)(tree.pass_up)
        pl.when(g == steps // 2)(tree.turn)
        pl.when(g == steps * 3 // 4)(tree.release)
        cin_pair(
            FIELDS, g, e_ref, c1_ref, c2_ref, top_ref, w1f_ref, w2f_ref, w2b_ref, w1b_ref, grads, *scratch
        )
        return carry

    lax.fori_loop(0, steps, cin_step, 0)

    g = jnp.concatenate(halves(grads[...].reshape(count, width)), axis=1)
    merged = []
    for b in range(listed // 256):
        place = lax.broadcasted_iota(jnp.int32, (256, count), 0) + b * 256
        m = dot(jnp.where(place == inv_ref[...], 1.0, 0.0).astype(BF), g)
        merged.append(m[:, :width] + m[:, width:])
    merged = jnp.concatenate(halves(jnp.concatenate(merged, axis=0)), axis=1)
    for c in range(CAP):
        place = lax.broadcasted_iota(jnp.int32, (owners, listed), 0) + c * owners
        m = dot(jnp.where(place == target, 1.0, 0.0).astype(BF), merged)
        send[:, c, :] = m[:, :width] + m[:, width:]
    rows[me] = send[me]

    def send_rows(k, carry):
        group, member = moved((k * COPIES) % owners)
        pltpu.make_async_remote_copy(
            src_ref=send.at[group * 64 + member], dst_ref=rows.at[me],
            send_sem=rows_out, recv_sem=rows_in,
            device_id=(group, member), device_id_type=MESH,
        ).start()
        return carry

    lax.fori_loop(1, owners, send_rows, 0)
    others = pl.ds(0, owners - 1)
    pltpu.make_async_copy(send.at[others], rows.at[others], rows_in).wait()

    numbers = rows[:, CAP, :].T[:16].astype(jnp.int32)
    ask_v[...] = jnp.clip(numbers, 0, rows_dev - 1)
    to_scalars = pltpu.make_async_copy(ask_v, ask_s, own)
    to_scalars.start()
    for c in range(CAP):
        pair[c * owners : (c + 1) * owners, :] = jnp.concatenate(halves(rows[:, c, :]), axis=1)
    lane = lax.broadcasted_iota(jnp.int32, (128, 128), 1)
    table_copy.wait()
    for b in range(table_ref.shape[0] // 1024):
        for r in range(8):
            place = lax.broadcasted_iota(jnp.int32, (128, owners), 0) + (b * 1024 + r * 128)
            for c in range(CAP):
                hit = place == numbers[c : c + 1, :]
                hot[r * 128 : (r + 1) * 128, c * owners : (c + 1) * owners] = jnp.where(hit, 1.0, 0.0).astype(BF)
        s = dot(hot[...], pair[...])
        grad[...] = s[:, :width] + s[:, width:]
        means = jnp.zeros((128, 128), F32)
        for r in range(8):
            part = grad[r * 128 : (r + 1) * 128, :]
            means = jnp.where(lane == r, jnp.mean(part * part, axis=1, keepdims=True), means)
        na = accum_ref[8 * b : 8 * b + 8, :] + means.T[:8]
        na_ref[8 * b : 8 * b + 8, :] = na
        scale = RATE / (jnp.sqrt(na) + EPS)
        scale = jnp.concatenate([scale, jnp.zeros((120, 128), F32)], axis=0).T
        for r in range(8):
            at = slice(b * 1024 + r * 128, b * 1024 + (r + 1) * 128)
            nt_ref[at, :] = nt_ref[at, :] - grad[r * 128 : (r + 1) * 128, :] * scale[:, r : r + 1]
    to_scalars.wait()

    def look_up(p, out):
        for t in range(RCAP):
            row = jnp.clip(ask_s[8 + t, p], 0, rows_dev - 1)
            out[p, t : t + 1, :] = nt_ref[pl.ds(row, 1), :]

    late = 4

    def gather(k):
        group, member = moved((k * COPIES) % owners)
        look_up(group * 64 + member, found)

    def send_answers(k):
        group, member = moved((k * COPIES) % owners)
        pltpu.make_async_remote_copy(
            src_ref=found.at[group * 64 + member], dst_ref=answers_ref.at[me],
            send_sem=answers_out, recv_sem=answers_in,
            device_id=(group, member), device_id_type=MESH,
        ).start()

    def first(k, carry):
        gather(k)
        return carry

    def both(k, carry):
        gather(k)
        send_answers(k - late)
        return carry

    def last(k, carry):
        send_answers(k)
        return carry

    lax.fori_loop(1, 1 + late, first, 0)
    look_up(me, found)
    table_back = pltpu.make_async_copy(nt_ref, nt_out, table_out)
    table_back.start()
    lax.fori_loop(1 + late, owners, both, 0)
    mine = pltpu.make_async_copy(found.at[me], answers_ref.at[me], own)
    mine.start()
    lax.fori_loop(owners - late, owners, last, 0)
    mine.wait()
    table_back.wait()
    pltpu.make_async_copy(send.at[others], rows.at[others], rows_out).wait()
    pltpu.make_async_copy(found.at[others], answers_ref.at[others], answers_in).wait()
    pltpu.make_async_copy(found.at[others], answers_ref.at[others], answers_out).wait()


def step(inverse, unique_ids, next_ids, table, accum, operands):
    rows_dev, width = table.shape
    samples, fields = inverse.shape
    owners = lax.axis_size("group") * lax.axis_size("member")
    count = samples * FQ
    inv = jnp.pad(inverse, ((0, 0), (0, FQ - fields)), constant_values=-1).reshape(1, -1)
    vmem = pl.BlockSpec(memory_space=pltpu.VMEM)
    return pl.pallas_call(
        step_kernel,
        in_specs=[vmem] * 3 + [pl.BlockSpec(memory_space=pl.ANY)] + [vmem] * (1 + len(operands)),
        out_specs=[pl.BlockSpec(memory_space=pl.ANY), vmem, pl.BlockSpec(memory_space=pl.ANY)],
        out_shape=[
            jax.ShapeDtypeStruct(table.shape, F32),
            jax.ShapeDtypeStruct((rows_dev // 128, 128), F32),
            jax.ShapeDtypeStruct((owners, RCAP, width), F32),
        ],
        scratch_shapes=[
            pltpu.VMEM(table.shape, F32),
            pltpu.VMEM((1024, CAP * owners), BF),
            pltpu.VMEM((CAP * owners, 2 * width), BF),
            pltpu.VMEM((1024, width), F32),
            pltpu.VMEM((samples, FQ, width), F32),
            pltpu.VMEM((owners, CAP + 1, width), F32),
            pltpu.VMEM((owners, CAP + 1, width), F32),
            pltpu.VMEM((owners, RCAP, width), F32),
            pltpu.VMEM((16, owners), jnp.int32),
            pltpu.SMEM((16, owners), jnp.int32),
        ]
        + [pltpu.SemaphoreType.DMA] * 7
        + cin_scratch(fields),
        compiler_params=pltpu.CompilerParams(
            collective_id=0, has_side_effects=True, vmem_limit_bytes=56 << 20
        ),
        name="step",
    )(inv, unique_ids, next_ids, table, accum.reshape(rows_dev // 128, 128), *operands)


PIECES = 4


def finish_kernel(starts_ref, answers_ref, nt_ref, na_ref, out_ref, nt_out, na_out, answers, table, lines, sem, ins, outs):
    fetch = pltpu.make_async_copy(answers_ref, answers, sem)
    fetch.start()
    size = table.shape[0] // PIECES
    pieces = [pl.ds(k * size, size) for k in range(PIECES)]
    for k, at in enumerate(pieces):
        pltpu.make_async_copy(nt_ref.at[at], table.at[at], ins.at[k]).start()
    na_out[...] = na_ref[...]
    fetch.wait()
    for k, at in enumerate(pieces):
        pltpu.make_async_copy(nt_ref.at[at], table.at[at], ins.at[k]).wait()
        pltpu.make_async_copy(table.at[at], nt_out.at[at], outs.at[k]).start()

    def place(k, carry):
        for t in range(8):
            o = k * 8 + t
            lines[pl.ds(starts_ref[o], RCAP), :] = answers[o]
        return carry

    lax.fori_loop(0, answers.shape[0] // 8, place, 0)
    out_ref[...] = lines[: out_ref.shape[0], :]
    for k, at in enumerate(pieces):
        pltpu.make_async_copy(table.at[at], nt_out.at[at], outs.at[k]).wait()


def finish(starts, answers, new_table, new_accum, asked):
    vmem, free = pl.BlockSpec(memory_space=pltpu.VMEM), pl.BlockSpec(memory_space=pl.ANY)
    width = answers.shape[2]
    return pl.pallas_call(
        finish_kernel,
        in_specs=[pl.BlockSpec(memory_space=pltpu.SMEM), free, free, vmem],
        out_specs=[vmem, free, vmem],
        out_shape=[
            jax.ShapeDtypeStruct((asked, width), F32),
            jax.ShapeDtypeStruct(new_table.shape, F32),
            jax.ShapeDtypeStruct(new_accum.shape, F32),
        ],
        scratch_shapes=[
            pltpu.VMEM(answers.shape, F32),
            pltpu.VMEM(new_table.shape, F32),
            pltpu.VMEM((asked + RCAP, width), F32),
            pltpu.SemaphoreType.DMA,
            pltpu.SemaphoreType.DMA((PIECES,)),
            pltpu.SemaphoreType.DMA((PIECES,)),
        ],
        compiler_params=pltpu.CompilerParams(vmem_limit_bytes=60 << 20),
        name="finish",
    )(starts, answers, new_table, new_accum)


def local(
    embeddings,
    cot_first,
    cot_second,
    cot_third,
    w_first,
    w_second,
    w_third,
    unique_ids,
    inverse,
    table,
    accum,
    next_ids,
):
    owners = lax.axis_size("group") * lax.axis_size("member")
    operands = cin_operands(embeddings, cot_first, cot_second, cot_third, w_first, w_second, w_third)
    new_table, new_accum, answers = step(inverse, unique_ids, next_ids, table, accum, operands)
    firsts = jnp.arange(owners, dtype=jnp.int32)[:, None] * table.shape[0]
    starts = jnp.sum((next_ids < firsts).astype(jnp.int32), axis=1)
    returned, new_table, new_accum = finish(starts, answers, new_table, new_accum, next_ids.shape[1])
    return (new_table, new_accum.reshape(accum.shape), returned[None])


def solution(mesh):
    in_specs = (
        P(("group", "member"), None, None),
        P(("group", "member"), None),
        P(("group", "member"), None),
        P(("group", "member"), None),
        P(),
        P(),
        P(),
        P(("group", "member"), None),
        P(("group", "member"), None),
        P(("group", "member"), None),
        P(("group", "member")),
        P(("group", "member"), None),
    )
    out_specs = (
        P(("group", "member"), None),
        P(("group", "member")),
        P(("group", "member"), None, None),
    )
    return jax.shard_map(local, mesh=mesh, in_specs=in_specs, out_specs=out_specs, check_vma=False)
```

```python
import jax
import jax.numpy as jnp
from jax import lax
from jax.experimental import pallas as pl
from jax.experimental.pallas import tpu as pltpu
from jax.sharding import PartitionSpec as P

FIELDS = 39
CAP = 4
RCAP = 8
RATE = 0.5
EPS = 1e-08

BF = jnp.bfloat16
F32 = jnp.float32


def halves(x):
    hi = x.astype(BF)
    return hi, (x - hi.astype(F32)).astype(BF)


def dot(a, b):
    return jnp.dot(a, b, preferred_element_type=F32)


FP = 48
FQ = 40
HP = 112
HQ = 104
KP = 128
JC = 3
LANES = 256


def half(s):
    return slice(s * 128, (s + 1) * 128)


def cin_layouts(e_ref, c1_ref, c2_ref, w1t_ref, w2b_ref, wide, columns, w1f, w2f):
    fields, samples = e_ref.shape[0], e_ref.shape[1]
    for f in range(fields):
        wide[f * samples : (f + 1) * samples, :] = e_ref[f].astype(F32)
    wide[fields * samples :, :] = jnp.zeros((wide.shape[0] - fields * samples, 128), F32)
    for k, ref in enumerate((c1_ref, c2_ref)):
        columns[k * HP : (k + 1) * HP, :] = ref[...].astype(F32).T[:HP].astype(BF)
    for source, to in ((w1t_ref, w1f), (w2b_ref, w2f)):

        def turn(c, carry, source=source, to=to):
            at = pl.ds(pl.multiple_of(c * 128, 128), 128)
            to[:, at] = source[at, :].astype(F32).T[:HP].astype(BF)
            return carry

        lax.fori_loop(0, source.shape[0] // 128, turn, 0, unroll=5)


def cin_first(g, top_ref, w2b_ref, wide, columns, w1f, w2f, keep, p1, p2, l1f, mid, l2s, fill):
    ef, part, low, base = keep
    fields, samples = FIELDS, columns.shape[1]
    for s in range(2):
        ef[:, half(s)] = wide[pl.ds(2 * g + s, FQ, stride=samples), :]
    e = jnp.concatenate([ef[...], jnp.zeros((FP - FQ, LANES), F32)], axis=0).astype(BF)
    e3 = e.reshape(FP // 16, 16, LANES)

    def row16(i):
        return jnp.broadcast_to(ef[i : i + 1, :], (16, LANES)).astype(BF)

    chosen = lax.broadcasted_iota(jnp.int32, (samples, LANES), 0) - 2 * g
    chosen = chosen == lax.broadcasted_iota(jnp.int32, (samples, LANES), 1) // 128
    cots = dot(columns[...], jnp.where(chosen, 1.0, 0.0).astype(BF))
    next(fill, None)
    uppers = []
    for s in range(2):
        top, one = top_ref[2 * g + s].T, e[:, half(s)]
        hi, lo = halves(top)
        rest = (top - hi.astype(F32) - lo.astype(F32)).astype(BF)
        grad_two = dot(hi, one) + (dot(lo, one) + dot(rest, one))
        uppers.append((cots[HP:, half(s)] + grad_two).astype(BF))
    upper = jnp.concatenate(uppers, axis=1)
    upper = jnp.concatenate([upper, jnp.zeros((KP - HP, LANES), BF)], axis=0)
    next(fill, None)
    for i in range(fields):
        p1[i * FP : (i + 1) * FP, :] = (e3 * row16(i)[None]).reshape(FP, LANES)
        if i % 13 == 12:
            next(fill, None)
    l1 = dot(w1f[:, : fields * FP], p1[...]).astype(BF)
    l1f[...] = l1.astype(F32)
    l3 = l1.reshape(HP // 16, 16, LANES)
    for _ in fill:
        pass

    acc = [jnp.zeros((HQ // 8, 8, 128), F32) for _ in range(2)]
    done = 0
    for c in range(fields // JC):
        mid[c % 2] = dot(w2b_ref[c * JC * HP : (c + 1) * JC * HP, :], upper)
        for k in range(JC):
            j = c * JC + k
            p2[j * HP : (j + 1) * HP, :] = (l3 * row16(j)[None]).reshape(HP, LANES)
        ready = (c + 1) * JC * HP
        if c + 1 < fields // JC:
            ready = ready // 512 * 512
        if ready > done:
            piece = dot(w2f[:, done:ready], p2[done:ready, :])
            if done:
                piece = piece + l2s[...]
            l2s[...] = piece
            done = ready
        for s in range(2):
            one = l1f[:HQ, half(s)].reshape(HQ // 8, 8, 128)
            for k in range(JC):
                j = c * JC + k
                m = mid[c % 2, k * HP : k * HP + HQ, half(s)].reshape(HQ // 8, 8, 128)
                b = jnp.broadcast_to(ef[j : j + 1, half(s)], (8, 128))
                acc[s] = acc[s] + m * b[None]
                part[j, :, half(s)] = jnp.sum(m * one, axis=0)
    part[fields:, :, :] = jnp.zeros((FQ - fields, 8, LANES), F32)
    l2 = l2s[...].astype(BF)
    lower = jnp.concatenate([acc[s].reshape(HQ, 128) for s in range(2)], axis=1)
    lower = (cots[:HQ] + lower).astype(F32)
    low[...] = jnp.concatenate([lower, jnp.zeros((KP - HQ, LANES), F32)], axis=0).astype(BF)
    for s in range(2):
        hi, lo = halves(top_ref[2 * g + s])
        base[:, half(s)] = dot(hi, l2[:, half(s)]) + dot(lo, l2[:, half(s)])


def cin_last(g, w1b_ref, out_ref, keep, bot):
    ef, part, low, base = keep
    blocks = FQ // 8
    lower = jnp.concatenate([low[...], low[...]], axis=0)
    sums = [[base[8 * i : 8 * i + 8, half(s)] for i in range(blocks)] for s in range(2)]
    at = 0
    for b in range(blocks):
        rows = 8 * (b + 1)
        product = dot(w1b_ref[at : at + 8 * rows, :], lower)
        bot[b % 2, : 8 * rows, :] = product
        at += 8 * rows
        for s in range(2):
            es = ef[:rows, half(s)].reshape(b + 1, 8, 128)
            for k in range(8):
                j = b * 8 + k
                m = bot[b % 2, k * rows : (k + 1) * rows, half(s)].reshape(b + 1, 8, 128)
                part[j, :, half(s)] = part[j, :, half(s)] + jnp.sum(m * es, axis=0)
                one = jnp.broadcast_to(ef[j : j + 1, half(s)], (8, 128))
                for i in range(b):
                    sums[s][i] = sums[s][i] + m[i] * one
        yield
    for s in range(2):
        out_ref[2 * g + s] = jnp.sum(part[:, :, half(s)], axis=1) + jnp.concatenate(sums[s], axis=0)
        yield


def cin_all(
    between,
    e_ref, c1_ref, c2_ref, top_ref, w1t_ref, w2b_ref, w1b_ref, out_ref,
    wide, columns, w1f, w2f, p1, p2, l1f, mid, l2s, bot, *kept,
):
    keeps = (kept[:4], kept[4:])
    cin_layouts(e_ref, c1_ref, c2_ref, w1t_ref, w2b_ref, wide, columns, w1f, w2f)
    turns = columns.shape[1] // 4

    def turn(t, carry):
        between(t, turns)
        for k in range(2):
            g = 2 * t + k
            fill = cin_last(jnp.maximum(g - 1, 0), w1b_ref, out_ref, keeps[1 - k], bot)
            cin_first(
                g, top_ref, w2b_ref, wide, columns, w1f, w2f, keeps[k], p1, p2, l1f, mid, l2s, fill
            )
        return carry

    lax.fori_loop(0, turns, turn, 0)
    for _ in cin_last(2 * turns - 1, w1b_ref, out_ref, keeps[1], bot):
        pass


def cin_operands(embeddings, cot_first, cot_second, cot_third, w_first, w_second, w_third):
    maps, fields = w_first.shape[:2]
    e = jnp.transpose(embeddings, (1, 0, 2))

    def wide(cot):
        return jnp.pad(cot, ((0, 0), (0, KP - maps)))

    w_third = jnp.pad(w_third, ((0, 0), (0, HP - maps), (0, FP - fields)))
    top = jnp.einsum("hij,nh->nji", w_third, cot_third, preferred_element_type=F32)

    w2b = jnp.transpose(w_second, (2, 1, 0))
    w2b = jnp.pad(w2b, ((0, FQ - fields), (0, HP - maps), (0, KP - maps))).reshape(FQ * HP, KP)
    w1 = jnp.transpose(w_first, (1, 2, 0))
    w1t = jnp.pad(w1, ((0, FQ - fields), (0, FP - fields), (0, KP - maps))).reshape(FQ * FP, KP)
    both = w1.astype(F32)
    both = both + jnp.swapaxes(both, 0, 1)
    both = jnp.pad(both, ((0, FQ - fields), (0, FQ - fields), (0, KP - maps)))
    both = [both[8 * b : 8 * b + 8, : 8 * (b + 1)].reshape(-1, KP) for b in range(FQ // 8)]
    w1b = jnp.concatenate(halves(jnp.concatenate(both, axis=0)), axis=1)
    return e, wide(cot_first), wide(cot_second), top, w1t, w2b, w1b


def cin_scratch(samples):
    return [
        pltpu.VMEM((FQ * samples, 128), F32),
        pltpu.VMEM((2 * HP, samples), BF),
        pltpu.VMEM((HP, FQ * FP), BF),
        pltpu.VMEM((HP, FQ * HP), BF),
        pltpu.VMEM((FIELDS * FP, LANES), BF),
        pltpu.VMEM((FIELDS * HP, LANES), BF),
        pltpu.VMEM((HP, LANES), F32),
        pltpu.VMEM((2, JC * HP, LANES), F32),
        pltpu.VMEM((HP, LANES), F32),
        pltpu.VMEM((2, 8 * FQ, LANES), F32),
    ] + [
        pltpu.VMEM((FQ, LANES), F32),
        pltpu.VMEM((FQ, 8, LANES), F32),
        pltpu.VMEM((KP, LANES), BF),
        pltpu.VMEM((FP, LANES), F32),
    ] * 2


def ranks(row_list, capacity, rows_dev):
    owner = row_list // rows_dev
    lane = lax.broadcasted_iota(jnp.int32, owner.shape, 1)
    within = jnp.zeros_like(owner)
    for k in range(1, capacity):
        same = jnp.logical_and(pltpu.roll(owner, k, 1) == owner, lane >= k)
        within = within + jnp.where(same, 1, 0)
    return owner, within, row_list - owner * rows_dev


def by_owner(owner, within, inside, owners, capacity):
    hot = lax.broadcasted_iota(jnp.int32, (owners, owner.shape[1]), 0) == owner
    hot = jnp.where(hot, 1.0, 0.0).astype(BF)
    place = lax.broadcasted_iota(jnp.int32, (8, owner.shape[1]), 0)
    value = jnp.where(place == within, inside + 1, 0)
    high = value // 64
    value = jnp.concatenate([high.astype(F32), (value - high * 64).astype(F32)], axis=0).astype(BF)
    found = lax.dot_general(hot, value, (((1,), (1,)), ((), ())), preferred_element_type=F32)
    return found[:, :8] * 64 + found[:, 8:] - 1


MESH = pl.DeviceIdType.MESH
CLASSES = 4


def outward(k, middle):
    return middle + (1 - 2 * (k % 2)) * ((k + 1) // 2)


def moved(step):
    group, member = lax.axis_index("group"), lax.axis_index("member")
    x, z, core = member // 16, (member // 2) % 8, member % 2
    group = (group + outward(step // 64, 2)) % 4
    z = (z + outward((step // 8) % 8, 4)) % 8
    x = (x + outward((step // 2) % 4, 2)) % 4
    return group, x * 16 + z * 2 + (core + step + 1) % 2


class Tree:
    def __init__(self):
        self.sem = pltpu.get_barrier_semaphore()
        self.group, member = lax.axis_index("group"), lax.axis_index("member")
        self.x, self.rest = member // 16, member % 16
        top = self.group * 4 + self.x
        self.root = jnp.logical_and(top == 0, self.rest == 0)
        self.leader = jnp.logical_and(top != 0, self.rest == 0)

    def signal(self, group, member):
        pl.semaphore_signal(self.sem, inc=1, device_id=(group, member), device_id_type=MESH)

    def arrive(self):
        @pl.when(self.rest != 0)
        def _():
            self.signal(self.group, self.x * 16)

    def pass_up(self):
        @pl.when(self.leader)
        def _():
            pl.semaphore_wait(self.sem, 15)
            self.signal(0, 0)

    def turn(self):
        @pl.when(self.root)
        def _():
            pl.semaphore_wait(self.sem, 30)

            def tell(k, carry):
                self.signal(k // 4, (k % 4) * 16)
                return carry

            lax.fori_loop(1, 16, tell, 0)

    def release(self):
        @pl.when(jnp.logical_not(self.root))
        def _():
            pl.semaphore_wait(self.sem, 1)

        @pl.when(self.rest == 0)
        def _():
            def tell(k, carry):
                self.signal(self.group, self.x * 16 + k)
                return carry

            lax.fori_loop(1, 16, tell, 0)


def step_kernel(
    inv_ref, ids_ref, next_ref, table_ref, accum_ref,
    e_ref, c1_ref, c2_ref, top_ref, w1t_ref, w2b_ref, w1b_ref,
    nt_out, na_ref, answers_ref, starts_ref,
    nt_ref, hot, high, grad, grads, send, rows, found, ask_v, ask_s, rows_out, rows_in, answers_out, answers_in, own, table_in, table_out,
    *scratch,
):
    tree = Tree()
    tree.arrive()
    table_copy = pltpu.make_async_copy(table_ref, nt_ref, table_in)
    table_copy.start()
    grad[...] = jnp.zeros_like(grad)
    ask_v[...] = jnp.zeros_like(ask_v)
    owners, width = send.shape[0], send.shape[2]
    rows_dev = table_ref.shape[0]
    me = lax.axis_index("group") * 64 + lax.axis_index("member")
    count, listed = inv_ref.shape[1], ids_ref.shape[1]

    owner, within, inside = ranks(ids_ref[...], CAP, rows_dev)
    target = within * owners + owner
    ask_owner, ask_within, ask_inside = ranks(next_ref[...], RCAP, rows_dev)
    numbers = [
        by_owner(owner, within, inside, owners, CAP),
        by_owner(ask_owner, ask_within, ask_inside, owners, RCAP),
    ]
    send[:, CAP, :] = jnp.concatenate(numbers + [jnp.zeros((owners, width - 16), F32)], axis=1)
    before = ask_owner < lax.broadcasted_iota(jnp.int32, (owners, ask_owner.shape[1]), 0)
    starts = lax.dot_general(
        jnp.ones((16, ask_owner.shape[1]), BF), jnp.where(before, 1.0, 0.0).astype(BF),
        (((1,), (1,)), ((), ())), preferred_element_type=F32,
    )
    starts_ref[...] = starts[:8].astype(jnp.int32)

    def between(turn, turns):
        pl.when(turn == turns // 4)(tree.pass_up)
        pl.when(turn == turns // 2)(tree.turn)
        pl.when(turn == turns * 3 // 4)(tree.release)

    cin_all(
        between, e_ref, c1_ref, c2_ref, top_ref, w1t_ref, w2b_ref, w1b_ref, grads, *scratch
    )

    g = jnp.concatenate(halves(grads[...].reshape(count, width)), axis=1)
    merged = []
    for b in range(listed // 256):
        place = lax.broadcasted_iota(jnp.int32, (256, count), 0) + b * 256
        m = dot(jnp.where(place == inv_ref[...], 1.0, 0.0).astype(BF), g)
        merged.append(m[:, :width] + m[:, width:])
    merged = jnp.concatenate(halves(jnp.concatenate(merged, axis=0)), axis=1)
    for c in range(CAP):
        place = lax.broadcasted_iota(jnp.int32, (owners, listed), 0) + c * owners
        m = dot(jnp.where(place == target, 1.0, 0.0).astype(BF), merged)
        send[:, c, :] = m[:, :width] + m[:, width:]
    rows[me] = send[me]

    def send_rows(k, carry):
        to, member = moved(k)
        pltpu.make_async_remote_copy(
            src_ref=send.at[to * 64 + member], dst_ref=rows.at[me],
            send_sem=rows_out, recv_sem=rows_in.at[k // 64],
            device_id=(to, member), device_id_type=MESH,
        ).start()
        return carry

    lax.fori_loop(0, owners - 1, send_rows, 0)

    part = owners // CLASSES
    group = lax.axis_index("group")

    def arrived(c, count):
        origin = (group - outward(c, 2) + CLASSES) % CLASSES
        at = pl.ds(pl.multiple_of(origin * part, part), count)
        pltpu.make_async_copy(send.at[at], rows.at[at], rows_in.at[c]).wait()
        at = pl.ds(pl.multiple_of(origin * part, part), part)
        numbers = rows[at, CAP, :].T[:16, :part].astype(jnp.int32)
        ask_v[origin, :, :part] = jnp.clip(numbers, 0, rows_dev - 1)
        values = jnp.concatenate([rows[at, k, :] for k in range(CAP)], axis=0)
        row = jnp.concatenate([numbers[k : k + 1] for k in range(CAP)], axis=1)
        place = lax.broadcasted_iota(jnp.int32, (64, CAP * part), 0)
        high[...] = jnp.where(place == row // 64, 1.0, 0.0)
        low = jnp.where(place == row - row // 64 * 64, 1.0, 0.0).astype(BF)
        return jnp.concatenate(halves(values), axis=1), low.reshape(4, 16, CAP * part)

    def product(b, values, low):
        for k in range(16):
            one = jnp.broadcast_to(high[pl.ds(b * 16 + k, 1), :], (16, CAP * part)).astype(BF)
            hot[k * 64 : (k + 1) * 64, :] = (low * one[None]).reshape(64, CAP * part)
        s = dot(hot[...], values)
        return s[:, :width] + s[:, width:]

    blocks = rows_dev // 1024

    def add_class(c, carry):
        values, low = arrived(c, part)

        def block(b, carry):
            at = pl.ds(pl.multiple_of(b * 1024, 1024), 1024)
            s = product(b, values, low)
            grad[at, :] = grad[at, :] + s
            return carry

        lax.fori_loop(0, blocks, block, 0)
        return carry

    lax.fori_loop(0, CLASSES - 1, add_class, 0)
    values, low = arrived(CLASSES - 1, part - 1)
    to_scalars = pltpu.make_async_copy(ask_v, ask_s, own)
    to_scalars.start()
    table_copy.wait()
    lane = lax.broadcasted_iota(jnp.int32, (128, 128), 1)

    def update(b, carry):
        at = pl.ds(pl.multiple_of(b * 1024, 1024), 1024)
        g = grad[at, :] + product(b, values, low)
        grad[at, :] = g
        total = dot(jnp.concatenate(halves(g * g), axis=1), jnp.ones((2 * width, 128), BF))
        means = jnp.zeros((128, 128), F32)
        for r in range(8):
            means = jnp.where(lane == r, total[r * 128 : (r + 1) * 128] * (1 / width), means)
        few = pl.ds(pl.multiple_of(8 * b, 8), 8)
        na = accum_ref[few, :] + means.T[:8]
        na_ref[few, :] = na
        scale = RATE / (jnp.sqrt(na) + EPS)
        scale = jnp.concatenate([scale, jnp.zeros((120, 128), F32)], axis=0).T
        for r in range(8):
            at = pl.ds(pl.multiple_of(b * 1024 + r * 128, 128), 128)
            nt_ref[at, :] = nt_ref[at, :] - grad[at, :] * scale[:, r : r + 1]
        return carry

    lax.fori_loop(0, blocks, update, 0)
    to_scalars.wait()

    def look_up(p):
        for t in range(RCAP):
            row = jnp.clip(ask_s[p // part, 8 + t, p % part], 0, rows_dev - 1)
            found[p, t : t + 1, :] = nt_ref[pl.ds(row, 1), :]

    late = 4

    def gather(k):
        to, member = moved(k)
        look_up(to * 64 + member)

    def send_answers(k):
        to, member = moved(k)
        pltpu.make_async_remote_copy(
            src_ref=found.at[to * 64 + member], dst_ref=answers_ref.at[me],
            send_sem=answers_out, recv_sem=answers_in,
            device_id=(to, member), device_id_type=MESH,
        ).start()

    def first(k, carry):
        gather(k)
        return carry

    def both(k, carry):
        gather(k)
        send_answers(k - late)
        return carry

    def last(k, carry):
        send_answers(k)
        return carry

    lax.fori_loop(0, late, first, 0)
    look_up(me)
    table_back = pltpu.make_async_copy(nt_ref, nt_out, table_out)
    table_back.start()
    lax.fori_loop(late, owners - 1, both, 0)
    mine = pltpu.make_async_copy(found.at[me], answers_ref.at[me], own)
    mine.start()
    lax.fori_loop(owners - 1 - late, owners - 1, last, 0)
    mine.wait()
    table_back.wait()
    others = pl.ds(0, owners - 1)
    pltpu.make_async_copy(send.at[others], rows.at[others], rows_out).wait()
    pltpu.make_async_copy(found.at[others], answers_ref.at[others], answers_in).wait()
    pltpu.make_async_copy(found.at[others], answers_ref.at[others], answers_out).wait()


def step(inverse, unique_ids, next_ids, table, accum, operands):
    rows_dev, width = table.shape
    samples, fields = inverse.shape
    owners = lax.axis_size("group") * lax.axis_size("member")
    count = samples * FQ
    inv = jnp.pad(inverse, ((0, 0), (0, FQ - fields)), constant_values=-1).reshape(1, -1)
    vmem = pl.BlockSpec(memory_space=pltpu.VMEM)
    return pl.pallas_call(
        step_kernel,
        in_specs=[vmem] * 3 + [pl.BlockSpec(memory_space=pl.ANY)] + [vmem] * (1 + len(operands)),
        out_specs=[pl.BlockSpec(memory_space=pl.ANY), vmem, pl.BlockSpec(memory_space=pl.ANY), vmem],
        out_shape=[
            jax.ShapeDtypeStruct(table.shape, F32),
            jax.ShapeDtypeStruct((rows_dev // 128, 128), F32),
            jax.ShapeDtypeStruct((owners, RCAP, width), F32),
            jax.ShapeDtypeStruct((8, owners), jnp.int32),
        ],
        scratch_shapes=[
            pltpu.VMEM(table.shape, F32),
            pltpu.VMEM((1024, CAP * owners // CLASSES), BF),
            pltpu.VMEM((64, CAP * owners // CLASSES), F32),
            pltpu.VMEM(table.shape, F32),
            pltpu.VMEM((samples, FQ, width), F32),
            pltpu.VMEM((owners, CAP + 1, width), F32),
            pltpu.VMEM((owners, CAP + 1, width), F32),
            pltpu.VMEM((owners, RCAP, width), F32),
            pltpu.VMEM((CLASSES, 16, 128), jnp.int32),
            pltpu.SMEM((CLASSES, 16, 128), jnp.int32),
            pltpu.SemaphoreType.DMA,
            pltpu.SemaphoreType.DMA((CLASSES,)),
        ]
        + [pltpu.SemaphoreType.DMA] * 5
        + cin_scratch(samples),
        compiler_params=pltpu.CompilerParams(
            collective_id=0, has_side_effects=True, vmem_limit_bytes=56 << 20
        ),
        name="step",
    )(inv, unique_ids, next_ids, table, accum.reshape(rows_dev // 128, 128), *operands)


PIECES = 4


def finish_kernel(starts_ref, answers_ref, nt_ref, na_ref, out_ref, nt_out, na_out, answers, table, lines, sems):
    some, size = answers.shape[0] // PIECES, table.shape[0] // PIECES

    def fetch(k):
        at = pl.ds(k * some, some)
        return pltpu.make_async_copy(answers_ref.at[at], answers.at[at], sems.at[0, k])

    def table_in(k):
        at = pl.ds(k * size, size)
        return pltpu.make_async_copy(nt_ref.at[at], table.at[at], sems.at[1, k])

    def table_out(k):
        at = pl.ds(k * size, size)
        return pltpu.make_async_copy(table.at[at], nt_out.at[at], sems.at[2, k])

    for k in range(PIECES):
        fetch(k).start()
    for k in range(PIECES):
        table_in(k).start()
    na_out[...] = na_ref[...]

    def place(k, carry):
        for t in range(8):
            o = k * 8 + t
            lines[pl.ds(starts_ref[0, o], RCAP), :] = answers[o]
        return carry

    for k in range(PIECES):
        fetch(k).wait()
        lax.fori_loop(k * some // 8, (k + 1) * some // 8, place, 0)
        if k:
            table_in(k - 1).wait()
            table_out(k - 1).start()
    table_in(PIECES - 1).wait()
    table_out(PIECES - 1).start()
    result = pltpu.make_async_copy(lines.at[pl.ds(0, out_ref.shape[0])], out_ref, sems.at[3, 0])
    result.start()
    for k in range(PIECES):
        table_out(k).wait()
    result.wait()


def finish(starts, answers, new_table, new_accum, asked):
    vmem, free = pl.BlockSpec(memory_space=pltpu.VMEM), pl.BlockSpec(memory_space=pl.ANY)
    width = answers.shape[2]
    return pl.pallas_call(
        finish_kernel,
        in_specs=[pl.BlockSpec(memory_space=pltpu.SMEM), free, free, vmem],
        out_specs=[free, free, vmem],
        out_shape=[
            jax.ShapeDtypeStruct((asked, width), F32),
            jax.ShapeDtypeStruct(new_table.shape, F32),
            jax.ShapeDtypeStruct(new_accum.shape, F32),
        ],
        scratch_shapes=[
            pltpu.VMEM(answers.shape, F32),
            pltpu.VMEM(new_table.shape, F32),
            pltpu.VMEM((asked + RCAP, width), F32),
            pltpu.SemaphoreType.DMA((4, PIECES)),
        ],
        compiler_params=pltpu.CompilerParams(vmem_limit_bytes=60 << 20),
        name="finish",
    )(starts, answers, new_table, new_accum)


def local(
    embeddings,
    cot_first,
    cot_second,
    cot_third,
    w_first,
    w_second,
    w_third,
    unique_ids,
    inverse,
    table,
    accum,
    next_ids,
):
    operands = cin_operands(embeddings, cot_first, cot_second, cot_third, w_first, w_second, w_third)
    new_table, new_accum, answers, starts = step(inverse, unique_ids, next_ids, table, accum, operands)
    returned, new_table, new_accum = finish(starts, answers, new_table, new_accum, next_ids.shape[1])
    return (new_table, new_accum.reshape(accum.shape), returned[None])


def solution(mesh):
    in_specs = (
        P(("group", "member"), None, None),
        P(("group", "member"), None),
        P(("group", "member"), None),
        P(("group", "member"), None),
        P(),
        P(),
        P(),
        P(("group", "member"), None),
        P(("group", "member"), None),
        P(("group", "member"), None),
        P(("group", "member")),
        P(("group", "member"), None),
    )
    out_specs = (
        P(("group", "member"), None),
        P(("group", "member")),
        P(("group", "member"), None, None),
    )
    return jax.shard_map(local, mesh=mesh, in_specs=in_specs, out_specs=out_specs, check_vma=False)
```

```python
import jax
import jax.numpy as jnp
from jax import lax
from jax.experimental import pallas as pl
from jax.experimental.pallas import tpu as pltpu
from jax.sharding import PartitionSpec as P

FIELDS = 39
CAP = 4
RCAP = 8
RATE = 0.5
EPS = 1e-08

BF = jnp.bfloat16
F32 = jnp.float32


def halves(x):
    hi = x.astype(BF)
    return hi, (x - hi.astype(F32)).astype(BF)


def dot(a, b):
    return jnp.dot(a, b, preferred_element_type=F32)


FP = 48
FQ = 40
HP = 112
HQ = 104
KP = 128
JC = 3
LANES = 256


def half(s):
    return slice(s * 128, (s + 1) * 128)


def cin_layouts(e_ref, c1_ref, c2_ref, w1_ref, w2_ref, wide, columns, tops, w1t, w2b, w1f, w2f):
    fields, samples = e_ref.shape[0], e_ref.shape[1]
    maps = c1_ref.shape[1]
    for ref in (columns, tops, w1t, w2b):
        ref[...] = jnp.zeros_like(ref)
    for f in range(fields):
        w1t[f * FP : f * FP + fields, :maps] = w1_ref[f]
        w2b[f * HP : f * HP + maps, :maps] = w2_ref[f]
    for f in range(fields):
        wide[f * samples : (f + 1) * samples, :] = e_ref[f].astype(F32)
    wide[fields * samples :, :] = jnp.zeros((wide.shape[0] - fields * samples, 128), F32)
    for k, ref in enumerate((c1_ref, c2_ref)):
        columns[k * HP : k * HP + maps, :] = ref[...].astype(F32).T.astype(BF)
    for source, to in ((w1t, w1f), (w2b, w2f)):

        def turn(c, carry, source=source, to=to):
            at = pl.ds(pl.multiple_of(c * 128, 128), 128)
            to[:, at] = source[at, :].astype(F32).T[:HP].astype(BF)
            return carry

        lax.fori_loop(0, source.shape[0] // 128, turn, 0, unroll=5)


def cin_first(g, top_ref, w2b_ref, wide, columns, tops, w1f, w2f, keep, p1, p2, l1f, mid, l2s, fill):
    ef, part, low, base = keep
    fields, samples = FIELDS, columns.shape[1]
    for s in range(2):
        ef[:, half(s)] = wide[pl.ds(2 * g + s, FQ, stride=samples), :]
    e = jnp.concatenate([ef[...], jnp.zeros((FP - FQ, LANES), F32)], axis=0).astype(BF)
    e3 = e.reshape(FP // 16, 16, LANES)

    def row16(i):
        return jnp.broadcast_to(ef[i : i + 1, :], (16, LANES)).astype(BF)

    chosen = lax.broadcasted_iota(jnp.int32, (samples, LANES), 0) - 2 * g
    chosen = chosen == lax.broadcasted_iota(jnp.int32, (samples, LANES), 1) // 128
    cots = dot(columns[...], jnp.where(chosen, 1.0, 0.0).astype(BF))
    next(fill, None)
    uppers = []
    for s in range(2):
        tops[s, :fields, : top_ref.shape[2]] = top_ref[2 * g + s]
        top, one = tops[s].T[:HP], e[:, half(s)]
        hi, lo = halves(top)
        rest = (top - hi.astype(F32) - lo.astype(F32)).astype(BF)
        grad_two = dot(hi, one) + (dot(lo, one) + dot(rest, one))
        uppers.append((cots[HP:, half(s)] + grad_two).astype(BF))
    upper = jnp.concatenate(uppers, axis=1)
    upper = jnp.concatenate([upper, jnp.zeros((KP - HP, LANES), BF)], axis=0)
    next(fill, None)
    for i in range(fields):
        p1[i * FP : (i + 1) * FP, :] = (e3 * row16(i)[None]).reshape(FP, LANES)
        if i % 13 == 12:
            next(fill, None)
    l1 = dot(w1f[:, : fields * FP], p1[...]).astype(BF)
    l1f[...] = l1.astype(F32)
    l3 = l1.reshape(HP // 16, 16, LANES)
    for _ in fill:
        pass

    acc = [jnp.zeros((HQ // 8, 8, 128), F32) for _ in range(2)]
    done = 0
    for c in range(fields // JC):
        mid[c % 2] = dot(w2b_ref[c * JC * HP : (c + 1) * JC * HP, :], upper)
        for k in range(JC):
            j = c * JC + k
            p2[j * HP : (j + 1) * HP, :] = (l3 * row16(j)[None]).reshape(HP, LANES)
        ready = (c + 1) * JC * HP
        if c + 1 < fields // JC:
            ready = ready // 512 * 512
        if ready > done:
            piece = dot(w2f[:, done:ready], p2[done:ready, :])
            if done:
                piece = piece + l2s[...]
            l2s[...] = piece
            done = ready
        for s in range(2):
            one = l1f[:HQ, half(s)].reshape(HQ // 8, 8, 128)
            for k in range(JC):
                j = c * JC + k
                m = mid[c % 2, k * HP : k * HP + HQ, half(s)].reshape(HQ // 8, 8, 128)
                b = jnp.broadcast_to(ef[j : j + 1, half(s)], (8, 128))
                acc[s] = acc[s] + m * b[None]
                part[j, :, half(s)] = jnp.sum(m * one, axis=0)
    part[fields:, :, :] = jnp.zeros((FQ - fields, 8, LANES), F32)
    l2 = l2s[...].astype(BF)
    lower = jnp.concatenate([acc[s].reshape(HQ, 128) for s in range(2)], axis=1)
    lower = (cots[:HQ] + lower).astype(F32)
    low[...] = jnp.concatenate([lower, jnp.zeros((KP - HQ, LANES), F32)], axis=0).astype(BF)
    for s in range(2):
        hi, lo = halves(tops[s][:, :HP])
        base[:, half(s)] = dot(hi, l2[:, half(s)]) + dot(lo, l2[:, half(s)])


def cin_last(g, w1b_ref, out_ref, keep, bot):
    ef, part, low, base = keep
    blocks = FQ // 8
    lower = jnp.concatenate([low[...], low[...]], axis=0)
    sums = [[base[8 * i : 8 * i + 8, half(s)] for i in range(blocks)] for s in range(2)]
    at = 0
    for b in range(blocks):
        rows = 8 * (b + 1)
        product = dot(w1b_ref[at : at + 8 * rows, :], lower)
        bot[b % 2, : 8 * rows, :] = product
        at += 8 * rows
        for s in range(2):
            es = ef[:rows, half(s)].reshape(b + 1, 8, 128)
            for k in range(8):
                j = b * 8 + k
                m = bot[b % 2, k * rows : (k + 1) * rows, half(s)].reshape(b + 1, 8, 128)
                part[j, :, half(s)] = part[j, :, half(s)] + jnp.sum(m * es, axis=0)
                one = jnp.broadcast_to(ef[j : j + 1, half(s)], (8, 128))
                for i in range(b):
                    sums[s][i] = sums[s][i] + m[i] * one
        yield
    for s in range(2):
        out_ref[2 * g + s] = jnp.sum(part[:, :, half(s)], axis=1) + jnp.concatenate(sums[s], axis=0)
        yield


def cin_all(
    between,
    e_ref, c1_ref, c2_ref, top_ref, w1_ref, w2_ref, w1b_ref, out_ref,
    wide, columns, tops, w1t, w2b, w1f, w2f, p1, p2, l1f, mid, l2s, bot, *kept,
):
    keeps = (kept[:4], kept[4:])
    cin_layouts(e_ref, c1_ref, c2_ref, w1_ref, w2_ref, wide, columns, tops, w1t, w2b, w1f, w2f)
    turns = columns.shape[1] // 4

    def turn(t, carry):
        between(t, turns)
        for k in range(2):
            g = 2 * t + k
            fill = cin_last(jnp.maximum(g - 1, 0), w1b_ref, out_ref, keeps[1 - k], bot)
            cin_first(
                g, top_ref, w2b, wide, columns, tops, w1f, w2f, keeps[k], p1, p2, l1f, mid, l2s, fill
            )
        return carry

    lax.fori_loop(0, turns, turn, 0)
    for _ in cin_last(2 * turns - 1, w1b_ref, out_ref, keeps[1], bot):
        pass


def cin_operands(embeddings, cot_first, cot_second, cot_third, w_first, w_second, w_third):
    maps, fields = w_first.shape[:2]
    e = jnp.transpose(embeddings, (1, 0, 2))

    top = jnp.einsum("hij,nh->nji", w_third, cot_third, preferred_element_type=F32)
    w2 = jnp.transpose(w_second, (2, 1, 0))
    w1 = jnp.transpose(w_first, (1, 2, 0))
    both = w1.astype(F32)
    both = both + jnp.swapaxes(both, 0, 1)
    both = jnp.pad(both, ((0, FQ - fields), (0, FQ - fields), (0, KP - maps)))
    both = [both[8 * b : 8 * b + 8, : 8 * (b + 1)].reshape(-1, KP) for b in range(FQ // 8)]
    w1b = jnp.concatenate(halves(jnp.concatenate(both, axis=0)), axis=1)
    return e, cot_first, cot_second, top, w1, w2, w1b


def cin_scratch(samples):
    return [
        pltpu.VMEM((FQ * samples, 128), F32),
        pltpu.VMEM((2 * HP, samples), BF),
        pltpu.VMEM((2, FP, 128), F32),
        pltpu.VMEM((FQ * FP, KP), BF),
        pltpu.VMEM((FQ * HP, KP), BF),
        pltpu.VMEM((HP, FQ * FP), BF),
        pltpu.VMEM((HP, FQ * HP), BF),
        pltpu.VMEM((FIELDS * FP, LANES), BF),
        pltpu.VMEM((FIELDS * HP, LANES), BF),
        pltpu.VMEM((HP, LANES), F32),
        pltpu.VMEM((2, JC * HP, LANES), F32),
        pltpu.VMEM((HP, LANES), F32),
        pltpu.VMEM((2, 8 * FQ, LANES), F32),
    ] + [
        pltpu.VMEM((FQ, LANES), F32),
        pltpu.VMEM((FQ, 8, LANES), F32),
        pltpu.VMEM((KP, LANES), BF),
        pltpu.VMEM((FP, LANES), F32),
    ] * 2


def ranks(row_list, capacity, rows_dev):
    owner = row_list // rows_dev
    lane = lax.broadcasted_iota(jnp.int32, owner.shape, 1)
    within = jnp.zeros_like(owner)
    for k in range(1, capacity):
        same = jnp.logical_and(pltpu.roll(owner, k, 1) == owner, lane >= k)
        within = within + jnp.where(same, 1, 0)
    return owner, within, row_list - owner * rows_dev


def by_owner(owner, within, inside, owners, capacity):
    hot = lax.broadcasted_iota(jnp.int32, (owners, owner.shape[1]), 0) == owner
    hot = jnp.where(hot, 1.0, 0.0).astype(BF)
    place = lax.broadcasted_iota(jnp.int32, (8, owner.shape[1]), 0)
    value = jnp.where(place == within, inside + 1, 0)
    high = value // 64
    value = jnp.concatenate([high.astype(F32), (value - high * 64).astype(F32)], axis=0).astype(BF)
    found = lax.dot_general(hot, value, (((1,), (1,)), ((), ())), preferred_element_type=F32)
    return found[:, :8] * 64 + found[:, 8:] - 1


MESH = pl.DeviceIdType.MESH
CLASSES = 4


def outward(k, middle):
    return middle + (1 - 2 * (k % 2)) * ((k + 1) // 2)


class Peers:
    def __init__(self):
        self.group, member = lax.axis_index("group"), lax.axis_index("member")
        x, self.z, core = member // 16, (member // 2) % 8, member % 2
        self.near = [
            ((x + dx) % 4) * 16 + (core + dc) % 2 for dx in (2, 1, 3, 0) for dc in (1, 0)
        ]
        self.steps = 32

    def at(self, step):
        to = (self.group + outward(step // 8, 2)) % 4
        first = ((self.z + outward(step % 8, 4)) % 8) * 2
        return to, [first + n for n in self.near]


class Tree:
    def __init__(self):
        self.sem = pltpu.get_barrier_semaphore()
        self.group, member = lax.axis_index("group"), lax.axis_index("member")
        self.x, self.rest = member // 16, member % 16
        top = self.group * 4 + self.x
        self.root = jnp.logical_and(top == 0, self.rest == 0)
        self.leader = jnp.logical_and(top != 0, self.rest == 0)

    def signal(self, group, member):
        pl.semaphore_signal(self.sem, inc=1, device_id=(group, member), device_id_type=MESH)

    def arrive(self):
        @pl.when(self.rest != 0)
        def _():
            self.signal(self.group, self.x * 16)

    def pass_up(self):
        @pl.when(self.leader)
        def _():
            pl.semaphore_wait(self.sem, 15)
            self.signal(0, 0)

    def turn(self):
        @pl.when(self.root)
        def _():
            pl.semaphore_wait(self.sem, 30)

            def tell(k, carry):
                self.signal(k // 4, (k % 4) * 16)
                return carry

            lax.fori_loop(1, 16, tell, 0)

    def release(self):
        @pl.when(jnp.logical_not(self.root))
        def _():
            pl.semaphore_wait(self.sem, 1)

        @pl.when(self.rest == 0)
        def _():
            def tell(k, carry):
                self.signal(self.group, self.x * 16 + k)
                return carry

            lax.fori_loop(1, 16, tell, 0)


def step_kernel(
    inv_ref, ids_ref, next_ref, table_ref, accum_ref,
    e_ref, c1_ref, c2_ref, top_ref, w1_ref, w2_ref, w1b_ref,
    nt_out, na_ref, answers_ref, starts_ref,
    nt_ref, hot, high, grad, grads, send, rows, found, ask_v, ask_s, rows_out, rows_in, answers_out, answers_in, own, table_in, table_out,
    *scratch,
):
    tree = Tree()
    tree.arrive()
    table_copy = pltpu.make_async_copy(table_ref, nt_ref, table_in)
    table_copy.start()
    grad[...] = jnp.zeros_like(grad)
    ask_v[...] = jnp.zeros_like(ask_v)
    owners, width = send.shape[0], send.shape[2]
    rows_dev = table_ref.shape[0]
    me = lax.axis_index("group") * 64 + lax.axis_index("member")
    count, listed = inv_ref.shape[1], ids_ref.shape[1]

    owner, within, inside = ranks(ids_ref[...], CAP, rows_dev)
    target = within * owners + owner
    ask_owner, ask_within, ask_inside = ranks(next_ref[...], RCAP, rows_dev)
    numbers = [
        by_owner(owner, within, inside, owners, CAP),
        by_owner(ask_owner, ask_within, ask_inside, owners, RCAP),
    ]
    send[:, CAP, :] = jnp.concatenate(numbers + [jnp.zeros((owners, width - 16), F32)], axis=1)
    before = ask_owner < lax.broadcasted_iota(jnp.int32, (owners, ask_owner.shape[1]), 0)
    starts = lax.dot_general(
        jnp.ones((16, ask_owner.shape[1]), BF), jnp.where(before, 1.0, 0.0).astype(BF),
        (((1,), (1,)), ((), ())), preferred_element_type=F32,
    )
    starts_ref[...] = starts[:8].astype(jnp.int32)

    def between(turn, turns):
        pl.when(turn == turns // 4)(tree.pass_up)
        pl.when(turn == turns // 2)(tree.turn)
        pl.when(turn == turns * 3 // 4)(tree.release)

    cin_all(
        between, e_ref, c1_ref, c2_ref, top_ref, w1_ref, w2_ref, w1b_ref, grads, *scratch
    )

    g = jnp.concatenate(halves(grads[...].reshape(count, width)), axis=1)
    merged = []
    for b in range(listed // 256):
        place = lax.broadcasted_iota(jnp.int32, (256, count), 0) + b * 256
        m = dot(jnp.where(place == inv_ref[...], 1.0, 0.0).astype(BF), g)
        merged.append(m[:, :width] + m[:, width:])
    merged = jnp.concatenate(halves(jnp.concatenate(merged, axis=0)), axis=1)
    for c in range(CAP):
        place = lax.broadcasted_iota(jnp.int32, (owners, listed), 0) + c * owners
        m = dot(jnp.where(place == target, 1.0, 0.0).astype(BF), merged)
        send[:, c, :] = m[:, :width] + m[:, width:]
    rows[me] = send[me]

    peers = Peers()

    def send_rows(step, count=8):
        to, members = peers.at(step)
        for member in members[:count]:
            pltpu.make_async_remote_copy(
                src_ref=send.at[to * 64 + member], dst_ref=rows.at[me],
                send_sem=rows_out, recv_sem=rows_in.at[step // 8],
                device_id=(to, member), device_id_type=MESH,
            ).start()

    lax.fori_loop(0, peers.steps - 1, lambda step, carry: (send_rows(step), carry)[1], 0)
    send_rows(peers.steps - 1, 7)

    part = owners // CLASSES
    group = lax.axis_index("group")

    def arrived(c, count):
        origin = (group - outward(c, 2) + CLASSES) % CLASSES
        at = pl.ds(pl.multiple_of(origin * part, part), count)
        pltpu.make_async_copy(send.at[at], rows.at[at], rows_in.at[c]).wait()
        at = pl.ds(pl.multiple_of(origin * part, part), part)
        numbers = rows[at, CAP, :].T[:16, :part].astype(jnp.int32)
        ask_v[origin, :, :part] = jnp.clip(numbers, 0, rows_dev - 1)
        values = jnp.concatenate([rows[at, k, :] for k in range(CAP)], axis=0)
        row = jnp.concatenate([numbers[k : k + 1] for k in range(CAP)], axis=1)
        place = lax.broadcasted_iota(jnp.int32, (64, CAP * part), 0)
        high[...] = jnp.where(place == row // 64, 1.0, 0.0)
        low = jnp.where(place == row - row // 64 * 64, 1.0, 0.0).astype(BF)
        return jnp.concatenate(halves(values), axis=1), low.reshape(4, 16, CAP * part)

    def product(b, values, low):
        for k in range(16):
            one = jnp.broadcast_to(high[pl.ds(b * 16 + k, 1), :], (16, CAP * part)).astype(BF)
            hot[k * 64 : (k + 1) * 64, :] = (low * one[None]).reshape(64, CAP * part)
        s = dot(hot[...], values)
        return s[:, :width] + s[:, width:]

    blocks = rows_dev // 1024

    def add_class(c, carry):
        values, low = arrived(c, part)

        def block(b, carry):
            at = pl.ds(pl.multiple_of(b * 1024, 1024), 1024)
            s = product(b, values, low)
            grad[at, :] = grad[at, :] + s
            return carry

        lax.fori_loop(0, blocks, block, 0)
        return carry

    lax.fori_loop(0, CLASSES - 1, add_class, 0)
    values, low = arrived(CLASSES - 1, part - 1)
    to_scalars = pltpu.make_async_copy(ask_v, ask_s, own)
    to_scalars.start()
    table_copy.wait()
    lane = lax.broadcasted_iota(jnp.int32, (128, 128), 1)

    def update(b, carry):
        at = pl.ds(pl.multiple_of(b * 1024, 1024), 1024)
        g = grad[at, :] + product(b, values, low)
        grad[at, :] = g
        total = dot(jnp.concatenate(halves(g * g), axis=1), jnp.ones((2 * width, 128), BF))
        means = jnp.zeros((128, 128), F32)
        for r in range(8):
            means = jnp.where(lane == r, total[r * 128 : (r + 1) * 128] * (1 / width), means)
        few = pl.ds(pl.multiple_of(8 * b, 8), 8)
        na = accum_ref[few, :] + means.T[:8]
        na_ref[few, :] = na
        scale = RATE / (jnp.sqrt(na) + EPS)
        scale = jnp.concatenate([scale, jnp.zeros((120, 128), F32)], axis=0).T
        for r in range(8):
            at = pl.ds(pl.multiple_of(b * 1024 + r * 128, 128), 128)
            nt_ref[at, :] = nt_ref[at, :] - grad[at, :] * scale[:, r : r + 1]
        return carry

    lax.fori_loop(0, blocks, update, 0)
    to_scalars.wait()

    def gather(step):
        to, members = peers.at(step)
        for member in members:
            for t in range(RCAP):
                row = ask_s[to, 8 + t, member]
                found[to * 64 + member, t : t + 1, :] = nt_ref[pl.ds(row, 1), :]

    def send_answers(step, count=8):
        to, members = peers.at(step)
        for member in members[:count]:
            pltpu.make_async_remote_copy(
                src_ref=found.at[to * 64 + member], dst_ref=answers_ref.at[me],
                send_sem=answers_out, recv_sem=answers_in,
                device_id=(to, member), device_id_type=MESH,
            ).start()

    def both(step, carry):
        gather(step)
        send_answers(step - 1)
        return carry

    gather(0)
    lax.fori_loop(1, 4, both, 0)
    table_back = pltpu.make_async_copy(nt_ref, nt_out, table_out)
    table_back.start()
    lax.fori_loop(4, peers.steps, both, 0)
    send_answers(peers.steps - 1, 7)
    mine = pltpu.make_async_copy(found.at[me], answers_ref.at[me], own)
    mine.start()
    mine.wait()
    table_back.wait()
    others = pl.ds(0, owners - 1)
    pltpu.make_async_copy(send.at[others], rows.at[others], rows_out).wait()
    pltpu.make_async_copy(found.at[others], answers_ref.at[others], answers_in).wait()
    pltpu.make_async_copy(found.at[others], answers_ref.at[others], answers_out).wait()


def step(inverse, unique_ids, next_ids, table, accum, operands):
    rows_dev, width = table.shape
    samples, fields = inverse.shape
    owners = lax.axis_size("group") * lax.axis_size("member")
    count = samples * FQ
    inv = jnp.pad(inverse, ((0, 0), (0, FQ - fields)), constant_values=-1).reshape(1, -1)
    vmem = pl.BlockSpec(memory_space=pltpu.VMEM)
    return pl.pallas_call(
        step_kernel,
        in_specs=[vmem] * 3 + [pl.BlockSpec(memory_space=pl.ANY)] + [vmem] * (1 + len(operands)),
        out_specs=[pl.BlockSpec(memory_space=pl.ANY), vmem, pl.BlockSpec(memory_space=pl.ANY), vmem],
        out_shape=[
            jax.ShapeDtypeStruct(table.shape, F32),
            jax.ShapeDtypeStruct((rows_dev // 128, 128), F32),
            jax.ShapeDtypeStruct((owners, RCAP, width), F32),
            jax.ShapeDtypeStruct((8, owners), jnp.int32),
        ],
        scratch_shapes=[
            pltpu.VMEM(table.shape, F32),
            pltpu.VMEM((1024, CAP * owners // CLASSES), BF),
            pltpu.VMEM((64, CAP * owners // CLASSES), F32),
            pltpu.VMEM(table.shape, F32),
            pltpu.VMEM((samples, FQ, width), F32),
            pltpu.VMEM((owners, CAP + 1, width), F32),
            pltpu.VMEM((owners, CAP + 1, width), F32),
            pltpu.VMEM((owners, RCAP, width), F32),
            pltpu.VMEM((CLASSES, 16, 128), jnp.int32),
            pltpu.SMEM((CLASSES, 16, 128), jnp.int32),
            pltpu.SemaphoreType.DMA,
            pltpu.SemaphoreType.DMA((CLASSES,)),
        ]
        + [pltpu.SemaphoreType.DMA] * 5
        + cin_scratch(samples),
        compiler_params=pltpu.CompilerParams(
            collective_id=0, has_side_effects=True, vmem_limit_bytes=56 << 20
        ),
        name="step",
    )(inv, unique_ids, next_ids, table, accum.reshape(rows_dev // 128, 128), *operands)


PIECES = 4


def finish_kernel(starts_ref, answers_ref, nt_ref, na_ref, out_ref, nt_out, na_out, answers, table, lines, sems):
    some, size = answers.shape[0] // PIECES, table.shape[0] // PIECES

    def fetch(k):
        at = pl.ds(k * some, some)
        return pltpu.make_async_copy(answers_ref.at[at], answers.at[at], sems.at[0, k])

    def table_in(k):
        at = pl.ds(k * size, size)
        return pltpu.make_async_copy(nt_ref.at[at], table.at[at], sems.at[1, k])

    def table_out(k):
        at = pl.ds(k * size, size)
        return pltpu.make_async_copy(table.at[at], nt_out.at[at], sems.at[2, k])

    for k in range(PIECES):
        fetch(k).start()
    for k in range(PIECES):
        table_in(k).start()
    na_out[...] = na_ref[...]

    def place(k, carry):
        for t in range(8):
            o = k * 8 + t
            lines[pl.ds(starts_ref[0, o], RCAP), :] = answers[o]
        return carry

    for k in range(PIECES):
        fetch(k).wait()
        lax.fori_loop(k * some // 8, (k + 1) * some // 8, place, 0)
        if k:
            table_in(k - 1).wait()
            table_out(k - 1).start()
    table_in(PIECES - 1).wait()
    table_out(PIECES - 1).start()
    result = pltpu.make_async_copy(lines.at[pl.ds(0, out_ref.shape[0])], out_ref, sems.at[3, 0])
    result.start()
    for k in range(PIECES):
        table_out(k).wait()
    result.wait()


def finish(starts, answers, new_table, new_accum, asked):
    vmem, free = pl.BlockSpec(memory_space=pltpu.VMEM), pl.BlockSpec(memory_space=pl.ANY)
    width = answers.shape[2]
    return pl.pallas_call(
        finish_kernel,
        in_specs=[pl.BlockSpec(memory_space=pltpu.SMEM), free, free, vmem],
        out_specs=[free, free, vmem],
        out_shape=[
            jax.ShapeDtypeStruct((asked, width), F32),
            jax.ShapeDtypeStruct(new_table.shape, F32),
            jax.ShapeDtypeStruct(new_accum.shape, F32),
        ],
        scratch_shapes=[
            pltpu.VMEM(answers.shape, F32),
            pltpu.VMEM(new_table.shape, F32),
            pltpu.VMEM((asked + RCAP, width), F32),
            pltpu.SemaphoreType.DMA((4, PIECES)),
        ],
        compiler_params=pltpu.CompilerParams(vmem_limit_bytes=60 << 20),
        name="finish",
    )(starts, answers, new_table, new_accum)


def local(
    embeddings,
    cot_first,
    cot_second,
    cot_third,
    w_first,
    w_second,
    w_third,
    unique_ids,
    inverse,
    table,
    accum,
    next_ids,
):
    operands = cin_operands(embeddings, cot_first, cot_second, cot_third, w_first, w_second, w_third)
    new_table, new_accum, answers, starts = step(inverse, unique_ids, next_ids, table, accum, operands)
    returned, new_table, new_accum = finish(starts, answers, new_table, new_accum, next_ids.shape[1])
    return (new_table, new_accum.reshape(accum.shape), returned[None])


def solution(mesh):
    in_specs = (
        P(("group", "member"), None, None),
        P(("group", "member"), None),
        P(("group", "member"), None),
        P(("group", "member"), None),
        P(),
        P(),
        P(),
        P(("group", "member"), None),
        P(("group", "member"), None),
        P(("group", "member"), None),
        P(("group", "member")),
        P(("group", "member"), None),
    )
    out_specs = (
        P(("group", "member"), None),
        P(("group", "member")),
        P(("group", "member"), None, None),
    )
    return jax.shard_map(local, mesh=mesh, in_specs=in_specs, out_specs=out_specs, check_vma=False)
```

```python
import jax
import jax.numpy as jnp
from jax import lax
from jax.experimental import pallas as pl
from jax.experimental.pallas import tpu as pltpu
from jax.sharding import PartitionSpec as P

FIELDS = 39
CAP = 4
RCAP = 8
RATE = 0.5
EPS = 1e-08

BF = jnp.bfloat16
F32 = jnp.float32


def halves(x):
    hi = x.astype(BF)
    return hi, (x - hi.astype(F32)).astype(BF)


def dot(a, b):
    return jnp.dot(a, b, preferred_element_type=F32)


FP = 48
FQ = 40
HP = 112
HQ = 104
KP = 128
JC = 1
LANES = 256


def half(s):
    return slice(s * 128, (s + 1) * 128)


def cin_layouts(e_ref, c1_ref, c2_ref, w1_ref, w2_ref, wide, columns, tops, w1t, w2b, w1f, w2f):
    fields, samples = e_ref.shape[0], e_ref.shape[1]
    maps = c1_ref.shape[1]
    for ref in (columns, tops, w1t, w2b):
        ref[...] = jnp.zeros_like(ref)
    for f in range(fields):
        w1t[f * FP : f * FP + fields, :maps] = w1_ref[f]
        w2b[f * HP : f * HP + maps, :maps] = w2_ref[f]
    for f in range(fields):
        wide[f * samples : (f + 1) * samples, :] = e_ref[f].astype(F32)
    wide[fields * samples :, :] = jnp.zeros((wide.shape[0] - fields * samples, 128), F32)
    for k, ref in enumerate((c1_ref, c2_ref)):
        columns[k * HP : k * HP + maps, :] = ref[...].astype(F32).T.astype(BF)
    for source, to in ((w1t, w1f), (w2b, w2f)):

        def turn(c, carry, source=source, to=to):
            at = pl.ds(pl.multiple_of(c * 128, 128), 128)
            to[:, at] = source[at, :].astype(F32).T[:HP].astype(BF)
            return carry

        lax.fori_loop(0, source.shape[0] // 128, turn, 0, unroll=5)


def cin_first(g, top_ref, w2b_ref, wide, columns, tops, w1f, w2f, keep, p1, p2, l1f, mid, l2s, fill):
    ef, part, low, base = keep
    fields, samples = FIELDS, columns.shape[1]
    for s in range(2):
        ef[:, half(s)] = wide[pl.ds(2 * g + s, FQ, stride=samples), :]
    e = jnp.concatenate([ef[...], jnp.zeros((FP - FQ, LANES), F32)], axis=0).astype(BF)
    e3 = e.reshape(FP // 16, 16, LANES)

    def row16(i):
        return jnp.broadcast_to(ef[i : i + 1, :], (16, LANES)).astype(BF)

    chosen = lax.broadcasted_iota(jnp.int32, (samples, LANES), 0) - 2 * g
    chosen = chosen == lax.broadcasted_iota(jnp.int32, (samples, LANES), 1) // 128
    cots = dot(columns[...], jnp.where(chosen, 1.0, 0.0).astype(BF))
    next(fill, None)
    uppers = []
    for s in range(2):
        tops[s, :fields, : top_ref.shape[2]] = top_ref[2 * g + s]
        top, one = tops[s].T[:HP], e[:, half(s)]
        hi, lo = halves(top)
        rest = (top - hi.astype(F32) - lo.astype(F32)).astype(BF)
        grad_two = dot(hi, one) + (dot(lo, one) + dot(rest, one))
        uppers.append((cots[HP:, half(s)] + grad_two).astype(BF))
    upper = jnp.concatenate(uppers, axis=1)
    upper = jnp.concatenate([upper, jnp.zeros((KP - HP, LANES), BF)], axis=0)
    next(fill, None)
    for i in range(fields):
        p1[i * FP : (i + 1) * FP, :] = (e3 * row16(i)[None]).reshape(FP, LANES)
        if i % 13 == 12:
            next(fill, None)
    l1 = dot(w1f[:, : fields * FP], p1[...]).astype(BF)
    l1f[...] = l1.astype(F32)
    l3 = l1.reshape(HP // 16, 16, LANES)
    for _ in fill:
        pass

    acc = [jnp.zeros((HQ // 8, 8, 128), F32) for _ in range(2)]
    done = 0
    for c in range(fields // JC):
        mid[c % 2] = dot(w2b_ref[c * JC * HP : (c + 1) * JC * HP, :], upper)
        for k in range(JC):
            j = c * JC + k
            p2[j * HP : (j + 1) * HP, :] = (l3 * row16(j)[None]).reshape(HP, LANES)
        ready = (c + 1) * JC * HP
        if c + 1 < fields // JC:
            ready = ready // 512 * 512
        if ready > done:
            piece = dot(w2f[:, done:ready], p2[done:ready, :])
            if done:
                piece = piece + l2s[...]
            l2s[...] = piece
            done = ready
        for s in range(2):
            one = l1f[:HQ, half(s)].reshape(HQ // 8, 8, 128)
            for k in range(JC):
                j = c * JC + k
                m = mid[c % 2, k * HP : k * HP + HQ, half(s)].reshape(HQ // 8, 8, 128)
                b = jnp.broadcast_to(ef[j : j + 1, half(s)], (8, 128))
                acc[s] = acc[s] + m * b[None]
                part[j, :, half(s)] = jnp.sum(m * one, axis=0)
    part[fields:, :, :] = jnp.zeros((FQ - fields, 8, LANES), F32)
    l2 = l2s[...].astype(BF)
    lower = jnp.concatenate([acc[s].reshape(HQ, 128) for s in range(2)], axis=1)
    lower = (cots[:HQ] + lower).astype(F32)
    low[...] = jnp.concatenate([lower, jnp.zeros((KP - HQ, LANES), F32)], axis=0).astype(BF)
    for s in range(2):
        hi, lo = halves(tops[s][:, :HP])
        base[:, half(s)] = dot(hi, l2[:, half(s)]) + dot(lo, l2[:, half(s)])


def cin_last(g, w1b_ref, out_ref, keep, bot):
    ef, part, low, base = keep
    blocks = FQ // 8
    lower = jnp.concatenate([low[...], low[...]], axis=0)
    sums = [[base[8 * i : 8 * i + 8, half(s)] for i in range(blocks)] for s in range(2)]
    at = 0
    for b in range(blocks):
        rows = 8 * (b + 1)
        product = dot(w1b_ref[at : at + 8 * rows, :], lower)
        bot[b % 2, : 8 * rows, :] = product
        at += 8 * rows
        for s in range(2):
            es = ef[:rows, half(s)].reshape(b + 1, 8, 128)
            for k in range(8):
                j = b * 8 + k
                m = bot[b % 2, k * rows : (k + 1) * rows, half(s)].reshape(b + 1, 8, 128)
                part[j, :, half(s)] = part[j, :, half(s)] + jnp.sum(m * es, axis=0)
                one = jnp.broadcast_to(ef[j : j + 1, half(s)], (8, 128))
                for i in range(b):
                    sums[s][i] = sums[s][i] + m[i] * one
        yield
    for s in range(2):
        out_ref[2 * g + s] = jnp.sum(part[:, :, half(s)], axis=1) + jnp.concatenate(sums[s], axis=0)
        yield


def cin_all(
    between,
    e_ref, c1_ref, c2_ref, top_ref, w1_ref, w2_ref, w1b_ref, out_ref,
    wide, columns, tops, w1t, w2b, w1f, w2f, p1, p2, l1f, mid, l2s, bot, *kept,
):
    keeps = (kept[:4], kept[4:])
    cin_layouts(e_ref, c1_ref, c2_ref, w1_ref, w2_ref, wide, columns, tops, w1t, w2b, w1f, w2f)
    turns = columns.shape[1] // 4

    def turn(t, carry):
        between(t, turns)
        for k in range(2):
            g = 2 * t + k
            fill = cin_last(jnp.maximum(g - 1, 0), w1b_ref, out_ref, keeps[1 - k], bot)
            cin_first(
                g, top_ref, w2b, wide, columns, tops, w1f, w2f, keeps[k], p1, p2, l1f, mid, l2s, fill
            )
        return carry

    lax.fori_loop(0, turns, turn, 0)
    for _ in cin_last(2 * turns - 1, w1b_ref, out_ref, keeps[1], bot):
        pass


def cin_operands(embeddings, cot_first, cot_second, cot_third, w_first, w_second, w_third):
    maps, fields = w_first.shape[:2]
    e = jnp.transpose(embeddings, (1, 0, 2))

    top = jnp.einsum("hij,nh->nji", w_third, cot_third, preferred_element_type=F32)
    w2 = jnp.transpose(w_second, (2, 1, 0))
    w1 = jnp.transpose(w_first, (1, 2, 0))
    both = w1.astype(F32)
    both = both + jnp.swapaxes(both, 0, 1)
    both = jnp.pad(both, ((0, FQ - fields), (0, FQ - fields), (0, KP - maps)))
    both = [both[8 * b : 8 * b + 8, : 8 * (b + 1)].reshape(-1, KP) for b in range(FQ // 8)]
    w1b = jnp.concatenate(halves(jnp.concatenate(both, axis=0)), axis=1)
    return e, cot_first, cot_second, top, w1, w2, w1b


def cin_scratch(samples):
    return [
        pltpu.VMEM((FQ * samples, 128), F32),
        pltpu.VMEM((2 * HP, samples), BF),
        pltpu.VMEM((2, FP, 128), F32),
        pltpu.VMEM((FQ * FP, KP), BF),
        pltpu.VMEM((FQ * HP, KP), BF),
        pltpu.VMEM((HP, FQ * FP), BF),
        pltpu.VMEM((HP, FQ * HP), BF),
        pltpu.VMEM((FIELDS * FP, LANES), BF),
        pltpu.VMEM((FIELDS * HP, LANES), BF),
        pltpu.VMEM((HP, LANES), F32),
        pltpu.VMEM((2, JC * HP, LANES), F32),
        pltpu.VMEM((HP, LANES), F32),
        pltpu.VMEM((2, 8 * FQ, LANES), F32),
    ] + [
        pltpu.VMEM((FQ, LANES), F32),
        pltpu.VMEM((FQ, 8, LANES), F32),
        pltpu.VMEM((KP, LANES), BF),
        pltpu.VMEM((FP, LANES), F32),
    ] * 2


def ranks(row_list, capacity, rows_dev):
    owner = row_list // rows_dev
    lane = lax.broadcasted_iota(jnp.int32, owner.shape, 1)
    within = jnp.zeros_like(owner)
    for k in range(1, capacity):
        same = jnp.logical_and(pltpu.roll(owner, k, 1) == owner, lane >= k)
        within = within + jnp.where(same, 1, 0)
    return owner, within, row_list - owner * rows_dev


def by_owner(owner, within, inside, owners, capacity):
    hot = lax.broadcasted_iota(jnp.int32, (owners, owner.shape[1]), 0) == owner
    hot = jnp.where(hot, 1.0, 0.0).astype(BF)
    place = lax.broadcasted_iota(jnp.int32, (8, owner.shape[1]), 0)
    value = jnp.where(place == within, inside + 1, 0)
    high = value // 64
    value = jnp.concatenate([high.astype(F32), (value - high * 64).astype(F32)], axis=0).astype(BF)
    found = lax.dot_general(hot, value, (((1,), (1,)), ((), ())), preferred_element_type=F32)
    return found[:, :8] * 64 + found[:, 8:] - 1


MESH = pl.DeviceIdType.MESH
CLASSES = 4


def outward(k, middle):
    return middle + (1 - 2 * (k % 2)) * ((k + 1) // 2)


class Peers:
    def __init__(self):
        self.group, member = lax.axis_index("group"), lax.axis_index("member")
        x, self.z, core = member // 16, (member // 2) % 8, member % 2
        self.near = [
            ((x + dx) % 4) * 16 + (core + dc) % 2 for dx in (2, 1, 3, 0) for dc in (1, 0)
        ]
        self.steps = 32

    def at(self, step):
        to = (self.group + outward(step // 8, 2)) % 4
        first = ((self.z + outward(step % 8, 4)) % 8) * 2
        return to, [first + n for n in self.near]


def in_a_row(inverse, count):
    samples, fields = inverse.shape
    sample = (lax.broadcasted_iota(jnp.int32, (samples, count), 1) * 1639) // 65536
    own = sample == lax.broadcasted_iota(jnp.int32, (samples, count), 0)
    field = lax.broadcasted_iota(jnp.int32, (fields, count), 1)
    field = field - (field * 1639) // 65536 * FQ
    chosen = jnp.where(field == lax.broadcasted_iota(jnp.int32, (fields, count), 0), 1.0, 0.0).astype(BF)
    value = inverse + 1
    high = value // 64
    both = jnp.concatenate([high.astype(F32), (value - high * 64).astype(F32)], axis=0).astype(BF)
    spread = dot(both, chosen)
    spread = jnp.where(own, spread[:samples] * 64 + spread[samples:], 0.0)
    return jnp.sum(spread, axis=0, keepdims=True).astype(jnp.int32) - 1


class Tree:
    def __init__(self):
        self.sem = pltpu.get_barrier_semaphore()
        self.group, member = lax.axis_index("group"), lax.axis_index("member")
        self.x, self.rest = member // 16, member % 16
        top = self.group * 4 + self.x
        self.root = jnp.logical_and(top == 0, self.rest == 0)
        self.leader = jnp.logical_and(top != 0, self.rest == 0)

    def signal(self, group, member):
        pl.semaphore_signal(self.sem, inc=1, device_id=(group, member), device_id_type=MESH)

    def arrive(self):
        @pl.when(self.rest != 0)
        def _():
            self.signal(self.group, self.x * 16)

    def pass_up(self):
        @pl.when(self.leader)
        def _():
            pl.semaphore_wait(self.sem, 15)
            self.signal(0, 0)

    def turn(self):
        @pl.when(self.root)
        def _():
            pl.semaphore_wait(self.sem, 30)

            def tell(k, carry):
                self.signal(k // 4, (k % 4) * 16)
                return carry

            lax.fori_loop(1, 16, tell, 0)

    def release(self):
        @pl.when(jnp.logical_not(self.root))
        def _():
            pl.semaphore_wait(self.sem, 1)

        @pl.when(self.rest == 0)
        def _():
            def tell(k, carry):
                self.signal(self.group, self.x * 16 + k)
                return carry

            lax.fori_loop(1, 16, tell, 0)


def step_kernel(
    inv_ref, ids_ref, next_ref, table_ref, accum_ref,
    e_ref, c1_ref, c2_ref, top_ref, w1_ref, w2_ref, w1b_ref,
    nt_ref, na_ref, answers_ref, starts_ref,
    hot, high, grad, grads, send, rows, found, ask_v, ask_s, rows_out, rows_in, answers_out, answers_in, own, table_in,
    *scratch,
):
    tree = Tree()
    tree.arrive()
    table_copy = pltpu.make_async_copy(table_ref, nt_ref, table_in)
    table_copy.start()
    grad[...] = jnp.zeros_like(grad)
    ask_v[...] = jnp.zeros_like(ask_v)
    owners, width = send.shape[0], send.shape[2]
    rows_dev = table_ref.shape[0]
    me = lax.axis_index("group") * 64 + lax.axis_index("member")
    count, listed = grads.shape[0] * FQ, ids_ref.shape[1]
    positions = in_a_row(inv_ref[...], count)

    owner, within, inside = ranks(ids_ref[...], CAP, rows_dev)
    target = within * owners + owner
    ask_owner, ask_within, ask_inside = ranks(next_ref[...], RCAP, rows_dev)
    numbers = [
        by_owner(owner, within, inside, owners, CAP),
        by_owner(ask_owner, ask_within, ask_inside, owners, RCAP),
    ]
    send[:, CAP, :] = jnp.concatenate(numbers + [jnp.zeros((owners, width - 16), F32)], axis=1)
    before = ask_owner < lax.broadcasted_iota(jnp.int32, (owners, ask_owner.shape[1]), 0)
    starts = lax.dot_general(
        jnp.ones((16, ask_owner.shape[1]), BF), jnp.where(before, 1.0, 0.0).astype(BF),
        (((1,), (1,)), ((), ())), preferred_element_type=F32,
    )
    starts_ref[...] = starts[:8].astype(jnp.int32)

    def between(turn, turns):
        pl.when(turn == turns // 4)(tree.pass_up)
        pl.when(turn == turns // 2)(tree.turn)
        pl.when(turn == turns * 3 // 4)(tree.release)

    cin_all(
        between, e_ref, c1_ref, c2_ref, top_ref, w1_ref, w2_ref, w1b_ref, grads, *scratch
    )

    g = jnp.concatenate(halves(grads[...].reshape(count, width)), axis=1)
    merged = []
    for b in range(listed // 256):
        place = lax.broadcasted_iota(jnp.int32, (256, count), 0) + b * 256
        m = dot(jnp.where(place == positions, 1.0, 0.0).astype(BF), g)
        merged.append(m[:, :width] + m[:, width:])
    merged = jnp.concatenate(halves(jnp.concatenate(merged, axis=0)), axis=1)
    for c in range(CAP):
        place = lax.broadcasted_iota(jnp.int32, (owners, listed), 0) + c * owners
        m = dot(jnp.where(place == target, 1.0, 0.0).astype(BF), merged)
        send[:, c, :] = m[:, :width] + m[:, width:]
    rows[me] = send[me]

    peers = Peers()

    def send_rows(step, count=8):
        to, members = peers.at(step)
        for member in members[:count]:
            pltpu.make_async_remote_copy(
                src_ref=send.at[to * 64 + member], dst_ref=rows.at[me],
                send_sem=rows_out, recv_sem=rows_in.at[step // 8],
                device_id=(to, member), device_id_type=MESH,
            ).start()

    lax.fori_loop(0, peers.steps - 1, lambda step, carry: (send_rows(step), carry)[1], 0)
    send_rows(peers.steps - 1, 7)

    part = owners // CLASSES
    group = lax.axis_index("group")

    def arrived(c, count):
        origin = (group - outward(c, 2) + CLASSES) % CLASSES
        at = pl.ds(pl.multiple_of(origin * part, part), count)
        pltpu.make_async_copy(send.at[at], rows.at[at], rows_in.at[c]).wait()
        at = pl.ds(pl.multiple_of(origin * part, part), part)
        numbers = rows[at, CAP, :].T[:16, :part].astype(jnp.int32)
        ask_v[origin, :, :part] = jnp.clip(numbers, 0, rows_dev - 1)
        values = jnp.concatenate([rows[at, k, :] for k in range(CAP)], axis=0)
        row = jnp.concatenate([numbers[k : k + 1] for k in range(CAP)], axis=1)
        place = lax.broadcasted_iota(jnp.int32, (64, CAP * part), 0)
        high[...] = jnp.where(place == row // 64, 1.0, 0.0)
        low = jnp.where(place == row - row // 64 * 64, 1.0, 0.0).astype(BF)
        return jnp.concatenate(halves(values), axis=1), low.reshape(4, 16, CAP * part)

    def product(b, values, low):
        for k in range(16):
            one = jnp.broadcast_to(high[pl.ds(b * 16 + k, 1), :], (16, CAP * part)).astype(BF)
            hot[k * 64 : (k + 1) * 64, :] = (low * one[None]).reshape(64, CAP * part)
        s = dot(hot[...], values)
        return s[:, :width] + s[:, width:]

    blocks = rows_dev // 1024

    def add_class(c, carry):
        values, low = arrived(c, part)

        def block(b, carry):
            at = pl.ds(pl.multiple_of(b * 1024, 1024), 1024)
            s = product(b, values, low)
            grad[at, :] = grad[at, :] + s
            return carry

        lax.fori_loop(0, blocks, block, 0, unroll=2)
        return carry

    lax.fori_loop(0, CLASSES - 1, add_class, 0)
    values, low = arrived(CLASSES - 1, part - 1)
    to_scalars = pltpu.make_async_copy(ask_v, ask_s, own)
    to_scalars.start()
    table_copy.wait()
    lane = lax.broadcasted_iota(jnp.int32, (128, 128), 1)

    def update(b, carry):
        at = pl.ds(pl.multiple_of(b * 1024, 1024), 1024)
        g = grad[at, :] + product(b, values, low)
        grad[at, :] = g
        total = dot(jnp.concatenate(halves(g * g), axis=1), jnp.ones((2 * width, 128), BF))
        means = jnp.zeros((128, 128), F32)
        for r in range(8):
            means = jnp.where(lane == r, total[r * 128 : (r + 1) * 128] * (1 / width), means)
        few = pl.ds(pl.multiple_of(8 * b, 8), 8)
        na = accum_ref[few, :] + means.T[:8]
        na_ref[few, :] = na
        scale = RATE / (jnp.sqrt(na) + EPS)
        scale = jnp.concatenate([scale, jnp.zeros((120, 128), F32)], axis=0).T
        for r in range(8):
            at = pl.ds(pl.multiple_of(b * 1024 + r * 128, 128), 128)
            nt_ref[at, :] = nt_ref[at, :] - grad[at, :] * scale[:, r : r + 1]
        return carry

    lax.fori_loop(0, blocks, update, 0, unroll=True)
    to_scalars.wait()

    def gather(step):
        to, members = peers.at(step)
        for member in members:
            for t in range(RCAP):
                row = ask_s[to, 8 + t, member]
                found[to * 64 + member, t : t + 1, :] = nt_ref[pl.ds(row, 1), :]

    def send_answers(step, count=8):
        to, members = peers.at(step)
        for member in members[:count]:
            pltpu.make_async_remote_copy(
                src_ref=found.at[to * 64 + member], dst_ref=answers_ref.at[me],
                send_sem=answers_out, recv_sem=answers_in,
                device_id=(to, member), device_id_type=MESH,
            ).start()

    def both(step, carry):
        gather(step)
        send_answers(step - 1)
        return carry

    gather(0)
    lax.fori_loop(1, peers.steps, both, 0)
    send_answers(peers.steps - 1, 7)
    mine = pltpu.make_async_copy(found.at[me], answers_ref.at[me], own)
    mine.start()
    mine.wait()
    others = pl.ds(0, owners - 1)
    pltpu.make_async_copy(send.at[others], rows.at[others], rows_out).wait()
    pltpu.make_async_copy(found.at[others], answers_ref.at[others], answers_in).wait()
    pltpu.make_async_copy(found.at[others], answers_ref.at[others], answers_out).wait()


def step(inverse, unique_ids, next_ids, table, accum, operands):
    rows_dev, width = table.shape
    samples = inverse.shape[0]
    owners = lax.axis_size("group") * lax.axis_size("member")
    vmem = pl.BlockSpec(memory_space=pltpu.VMEM)
    return pl.pallas_call(
        step_kernel,
        in_specs=[vmem] * 3 + [pl.BlockSpec(memory_space=pl.ANY)] + [vmem] * (1 + len(operands)),
        out_specs=[vmem, vmem, vmem, vmem],
        out_shape=[
            pltpu.VMEM(table.shape, F32),
            pltpu.VMEM((rows_dev // 128, 128), F32),
            pltpu.VMEM((owners, RCAP, width), F32),
            pltpu.VMEM((8, owners), jnp.int32),
        ],
        scratch_shapes=[
            pltpu.VMEM((1024, CAP * owners // CLASSES), BF),
            pltpu.VMEM((64, CAP * owners // CLASSES), F32),
            pltpu.VMEM(table.shape, F32),
            pltpu.VMEM((samples, FQ, width), F32),
            pltpu.VMEM((owners, CAP + 1, width), F32),
            pltpu.VMEM((owners, CAP + 1, width), F32),
            pltpu.VMEM((owners, RCAP, width), F32),
            pltpu.VMEM((CLASSES, 16, 128), jnp.int32),
            pltpu.SMEM((CLASSES, 16, 128), jnp.int32),
            pltpu.SemaphoreType.DMA,
            pltpu.SemaphoreType.DMA((CLASSES,)),
        ]
        + [pltpu.SemaphoreType.DMA] * 4
        + cin_scratch(samples),
        compiler_params=pltpu.CompilerParams(
            collective_id=0, has_side_effects=True, vmem_limit_bytes=56 << 20
        ),
        name="step",
    )(inverse, unique_ids, next_ids, table, accum.reshape(rows_dev // 128, 128), *operands)


def finish_kernel(starts_ref, answers_ref, nt_ref, na_ref, out_ref, nt_out, na_out, lines, starts, sems):
    scalars = pltpu.make_async_copy(starts_ref, starts, sems.at[2])
    scalars.start()
    table = pltpu.make_async_copy(nt_ref, nt_out, sems.at[0])
    table.start()
    na_out[...] = na_ref[...]
    scalars.wait()

    def place(k, carry):
        for t in range(16):
            o = k * 16 + t
            lines[pl.ds(starts[0, o], RCAP), :] = answers_ref[o]
        return carry

    lax.fori_loop(0, answers_ref.shape[0] // 16, place, 0)
    result = pltpu.make_async_copy(lines.at[pl.ds(0, out_ref.shape[0])], out_ref, sems.at[1])
    result.start()
    table.wait()
    result.wait()


def finish(starts, answers, new_table, new_accum, asked):
    vmem, free = pl.BlockSpec(memory_space=pltpu.VMEM), pl.BlockSpec(memory_space=pl.ANY)
    width = answers.shape[2]
    return pl.pallas_call(
        finish_kernel,
        in_specs=[vmem] * 4,
        out_specs=[free, free, vmem],
        out_shape=[
            jax.ShapeDtypeStruct((asked, width), F32),
            jax.ShapeDtypeStruct(new_table.shape, F32),
            jax.ShapeDtypeStruct(new_accum.shape, F32),
        ],
        scratch_shapes=[
            pltpu.VMEM((asked + RCAP, width), F32),
            pltpu.SMEM(starts.shape, jnp.int32),
            pltpu.SemaphoreType.DMA((3,)),
        ],
        compiler_params=pltpu.CompilerParams(vmem_limit_bytes=8 << 20),
        name="finish",
    )(starts, answers, new_table, new_accum)


def local(
    embeddings,
    cot_first,
    cot_second,
    cot_third,
    w_first,
    w_second,
    w_third,
    unique_ids,
    inverse,
    table,
    accum,
    next_ids,
):
    operands = cin_operands(embeddings, cot_first, cot_second, cot_third, w_first, w_second, w_third)
    new_table, new_accum, answers, starts = step(inverse, unique_ids, next_ids, table, accum, operands)
    returned, new_table, new_accum = finish(starts, answers, new_table, new_accum, next_ids.shape[1])
    return (new_table, new_accum.reshape(accum.shape), returned[None])


def solution(mesh):
    in_specs = (
        P(("group", "member"), None, None),
        P(("group", "member"), None),
        P(("group", "member"), None),
        P(("group", "member"), None),
        P(),
        P(),
        P(),
        P(("group", "member"), None),
        P(("group", "member"), None),
        P(("group", "member"), None),
        P(("group", "member")),
        P(("group", "member"), None),
    )
    out_specs = (
        P(("group", "member"), None),
        P(("group", "member")),
        P(("group", "member"), None, None),
    )
    return jax.shard_map(local, mesh=mesh, in_specs=in_specs, out_specs=out_specs, check_vma=False)
```

```python
import jax
import jax.numpy as jnp
from jax import lax
from jax.experimental import pallas as pl
from jax.experimental.pallas import tpu as pltpu
from jax.sharding import PartitionSpec as P

FIELDS = 39
CAP = 4
RCAP = 8
RATE = 0.5
EPS = 1e-08

BF = jnp.bfloat16
F32 = jnp.float32


def halves(x):
    hi = x.astype(BF)
    return hi, (x - hi.astype(F32)).astype(BF)


def dot(a, b):
    return jnp.dot(a, b, preferred_element_type=F32)


FP = 48
FQ = 40
HP = 112
HQ = 104
KP = 128
JC = 1
LANES = 256


def half(s):
    return slice(s * 128, (s + 1) * 128)


def cin_layouts(e_ref, c1_ref, c2_ref, c3_ref, w1_ref, w2_ref, w3_ref, wide, columns, third, big, tops, w1t, w2b, w1f, w2f):
    fields, samples = e_ref.shape[0], e_ref.shape[1]
    maps = c1_ref.shape[1]
    for ref in (columns, third, big, tops, w1t, w2b):
        ref[...] = jnp.zeros_like(ref)
    third[:, :maps] = c3_ref[...]
    for f in range(fields):
        w1t[f * FP : f * FP + fields, :maps] = w1_ref[f]

    def widen(source):
        def one(k, carry):
            for t in range(10):
                h = k * 10 + t
                big[pl.ds(pl.multiple_of(h * FQ, 8), fields), :maps] = source[h].astype(F32)
            return carry

        lax.fori_loop(0, maps // 10, one, 0)

    widen(w3_ref)
    for f in range(fields):
        filters = big[pl.ds(f, HP, stride=FQ), :].astype(BF)
        tops[f * samples : (f + 1) * samples, :] = dot(third[:, :HP], filters)
    widen(w2_ref)
    for f in range(fields):
        w2b[f * HP : (f + 1) * HP, :HP] = big[pl.ds(f, HP, stride=FQ), :].T[:HP].astype(BF)
    for f in range(fields):
        wide[f * samples : (f + 1) * samples, :] = e_ref[f].astype(F32)
    wide[fields * samples :, :] = jnp.zeros((wide.shape[0] - fields * samples, 128), F32)
    for k, ref in enumerate((c1_ref, c2_ref)):
        columns[k * HP : k * HP + maps, :] = ref[...].astype(F32).T.astype(BF)
    for source, to in ((w1t, w1f), (w2b, w2f)):

        def turn(c, carry, source=source, to=to):
            at = pl.ds(pl.multiple_of(c * 128, 128), 128)
            to[:, at] = source[at, :].astype(F32).T[:HP].astype(BF)
            return carry

        lax.fori_loop(0, source.shape[0] // 128, turn, 0, unroll=True)


def cin_first(g, w2b_ref, wide, columns, tops, w1f, w2f, keep, p1, p2, l1f, mid, l2s, fill):
    ef, part, low, base = keep
    fields, samples = FIELDS, columns.shape[1]
    for s in range(2):
        ef[:, half(s)] = wide[pl.ds(2 * g + s, FQ, stride=samples), :]
    e = jnp.concatenate([ef[...], jnp.zeros((FP - FQ, LANES), F32)], axis=0).astype(BF)
    e3 = e.reshape(FP // 16, 16, LANES)

    def row16(i):
        return jnp.broadcast_to(ef[i : i + 1, :], (16, LANES)).astype(BF)

    chosen = lax.broadcasted_iota(jnp.int32, (samples, LANES), 0) - 2 * g
    chosen = chosen == lax.broadcasted_iota(jnp.int32, (samples, LANES), 1) // 128
    cots = dot(columns[...], jnp.where(chosen, 1.0, 0.0).astype(BF))
    next(fill, None)
    uppers = []
    for s in range(2):
        top, one = tops[pl.ds(2 * g + s, FP, stride=samples), :].T[:HP], e[:, half(s)]
        hi, lo = halves(top)
        rest = (top - hi.astype(F32) - lo.astype(F32)).astype(BF)
        grad_two = dot(hi, one) + (dot(lo, one) + dot(rest, one))
        uppers.append((cots[HP:, half(s)] + grad_two).astype(BF))
    upper = jnp.concatenate(uppers, axis=1)
    upper = jnp.concatenate([upper, jnp.zeros((KP - HP, LANES), BF)], axis=0)
    next(fill, None)
    for i in range(fields):
        p1[i * FP : (i + 1) * FP, :] = (e3 * row16(i)[None]).reshape(FP, LANES)
        if i % 13 == 12:
            next(fill, None)
    l1 = dot(w1f[:, : fields * FP], p1[...]).astype(BF)
    l1f[...] = l1.astype(F32)
    l3 = l1.reshape(HP // 16, 16, LANES)
    for _ in fill:
        pass

    acc = [jnp.zeros((HQ // 8, 8, 128), F32) for _ in range(2)]
    done = 0
    for c in range(fields // JC):
        mid[c % 2] = dot(w2b_ref[c * JC * HP : (c + 1) * JC * HP, :], upper)
        for k in range(JC):
            j = c * JC + k
            p2[j * HP : (j + 1) * HP, :] = (l3 * row16(j)[None]).reshape(HP, LANES)
        ready = (c + 1) * JC * HP
        if c + 1 < fields // JC:
            ready = ready // 1024 * 1024
        if ready > done:
            piece = dot(w2f[:, done:ready], p2[done:ready, :])
            if done:
                piece = piece + l2s[...]
            l2s[...] = piece
            done = ready
        for s in range(2):
            one = l1f[:HQ, half(s)].reshape(HQ // 8, 8, 128)
            for k in range(JC):
                j = c * JC + k
                m = mid[c % 2, k * HP : k * HP + HQ, half(s)].reshape(HQ // 8, 8, 128)
                b = jnp.broadcast_to(ef[j : j + 1, half(s)], (8, 128))
                acc[s] = acc[s] + m * b[None]
                part[j, :, half(s)] = jnp.sum(m * one, axis=0)
    part[fields:, :, :] = jnp.zeros((FQ - fields, 8, LANES), F32)
    l2 = l2s[...].astype(BF)
    lower = jnp.concatenate([acc[s].reshape(HQ, 128) for s in range(2)], axis=1)
    lower = (cots[:HQ] + lower).astype(F32)
    low[...] = jnp.concatenate([lower, jnp.zeros((KP - HQ, LANES), F32)], axis=0).astype(BF)
    for s in range(2):
        hi, lo = halves(tops[pl.ds(2 * g + s, FP, stride=samples), :][:, :HP])
        base[:, half(s)] = dot(hi, l2[:, half(s)]) + dot(lo, l2[:, half(s)])


def cin_last(g, w1b_ref, out_ref, keep, bot):
    ef, part, low, base = keep
    blocks = FQ // 8
    lower = jnp.concatenate([low[...], low[...]], axis=0)
    sums = [[base[8 * i : 8 * i + 8, half(s)] for i in range(blocks)] for s in range(2)]
    at = 0
    for b in range(blocks):
        rows = 8 * (b + 1)
        product = dot(w1b_ref[at : at + 8 * rows, :], lower)
        bot[b % 2, : 8 * rows, :] = product
        at += 8 * rows
        for s in range(2):
            es = ef[:rows, half(s)].reshape(b + 1, 8, 128)
            for k in range(8):
                j = b * 8 + k
                m = bot[b % 2, k * rows : (k + 1) * rows, half(s)].reshape(b + 1, 8, 128)
                part[j, :, half(s)] = part[j, :, half(s)] + jnp.sum(m * es, axis=0)
                one = jnp.broadcast_to(ef[j : j + 1, half(s)], (8, 128))
                for i in range(b):
                    sums[s][i] = sums[s][i] + m[i] * one
        yield
    for s in range(2):
        out_ref[2 * g + s] = jnp.sum(part[:, :, half(s)], axis=1) + jnp.concatenate(sums[s], axis=0)
        yield


def cin_all(
    between,
    e_ref, c1_ref, c2_ref, c3_ref, w1_ref, w2_ref, w3_ref, w1b_ref, out_ref,
    wide, columns, third, big, tops, w1t, w2b, w1f, w2f, p1, p2, l1f, mid, l2s, bot, *kept,
):
    keeps = (kept[:4], kept[4:])
    cin_layouts(
        e_ref, c1_ref, c2_ref, c3_ref, w1_ref, w2_ref, w3_ref, wide, columns, third, big, tops, w1t, w2b, w1f, w2f)
    turns = columns.shape[1] // 4

    def turn(t, carry):
        between(t, turns)
        for k in range(2):
            g = 2 * t + k
            fill = cin_last(jnp.maximum(g - 1, 0), w1b_ref, out_ref, keeps[1 - k], bot)
            cin_first(
                g, w2b, wide, columns, tops, w1f, w2f, keeps[k], p1, p2, l1f, mid, l2s, fill
            )
        return carry

    lax.fori_loop(0, turns, turn, 0)
    for _ in cin_last(2 * turns - 1, w1b_ref, out_ref, keeps[1], bot):
        pass


def cin_operands(embeddings, cot_first, cot_second, cot_third, w_first, w_second, w_third):
    maps, fields = w_first.shape[:2]
    e = jnp.transpose(embeddings, (1, 0, 2))

    w2, w3 = jnp.transpose(w_second, (0, 2, 1)), jnp.transpose(w_third, (0, 2, 1))
    w1 = jnp.transpose(w_first, (1, 2, 0))
    both = w1.astype(F32)
    both = both + jnp.swapaxes(both, 0, 1)
    both = jnp.pad(both, ((0, FQ - fields), (0, FQ - fields), (0, KP - maps)))
    both = [both[8 * b : 8 * b + 8, : 8 * (b + 1)].reshape(-1, KP) for b in range(FQ // 8)]
    w1b = jnp.concatenate(halves(jnp.concatenate(both, axis=0)), axis=1)
    return e, cot_first, cot_second, cot_third, w1, w2, w3, w1b


def cin_scratch(samples):
    return [
        pltpu.VMEM((FQ * samples, 128), F32),
        pltpu.VMEM((2 * HP, samples), BF),
        pltpu.VMEM((samples, 128), BF),
        pltpu.VMEM((HP * FQ, 128), F32),
        pltpu.VMEM((FP * samples, 128), F32),
        pltpu.VMEM((FQ * FP, KP), BF),
        pltpu.VMEM((FQ * HP, KP), BF),
        pltpu.VMEM((HP, FQ * FP), BF),
        pltpu.VMEM((HP, FQ * HP), BF),
        pltpu.VMEM((FIELDS * FP, LANES), BF),
        pltpu.VMEM((FIELDS * HP, LANES), BF),
        pltpu.VMEM((HP, LANES), F32),
        pltpu.VMEM((2, JC * HP, LANES), F32),
        pltpu.VMEM((HP, LANES), F32),
        pltpu.VMEM((2, 8 * FQ, LANES), F32),
    ] + [
        pltpu.VMEM((FQ, LANES), F32),
        pltpu.VMEM((FQ, 8, LANES), F32),
        pltpu.VMEM((KP, LANES), BF),
        pltpu.VMEM((FP, LANES), F32),
    ] * 2


def ranks(row_list, capacity, rows_dev):
    owner = row_list // rows_dev
    lane = lax.broadcasted_iota(jnp.int32, owner.shape, 1)
    within = jnp.zeros_like(owner)
    for k in range(1, capacity):
        same = jnp.logical_and(pltpu.roll(owner, k, 1) == owner, lane >= k)
        within = within + jnp.where(same, 1, 0)
    return owner, within, row_list - owner * rows_dev


def by_owner(owner, within, inside, owners, capacity):
    hot = lax.broadcasted_iota(jnp.int32, (owners, owner.shape[1]), 0) == owner
    hot = jnp.where(hot, 1.0, 0.0).astype(BF)
    place = lax.broadcasted_iota(jnp.int32, (8, owner.shape[1]), 0)
    value = jnp.where(place == within, inside + 1, 0)
    high = value // 64
    value = jnp.concatenate([high.astype(F32), (value - high * 64).astype(F32)], axis=0).astype(BF)
    found = lax.dot_general(hot, value, (((1,), (1,)), ((), ())), preferred_element_type=F32)
    return found[:, :8] * 64 + found[:, 8:] - 1


MESH = pl.DeviceIdType.MESH
CLASSES = 4


def outward(k, middle):
    return middle + (1 - 2 * (k % 2)) * ((k + 1) // 2)


class Peers:
    def __init__(self):
        self.group, member = lax.axis_index("group"), lax.axis_index("member")
        x, self.z, core = member // 16, (member // 2) % 8, member % 2
        self.near = [
            ((x + dx) % 4) * 16 + (core + dc) % 2 for dx in (2, 1, 3, 0) for dc in (1, 0)
        ]
        self.steps = 32

    def at(self, step):
        to = (self.group + outward(step // 8, 2)) % 4
        first = ((self.z + outward(step % 8, 4)) % 8) * 2
        return to, [first + n for n in self.near]


def in_a_row(inverse, count):
    samples, fields = inverse.shape
    sample = (lax.broadcasted_iota(jnp.int32, (samples, count), 1) * 1639) // 65536
    own = sample == lax.broadcasted_iota(jnp.int32, (samples, count), 0)
    field = lax.broadcasted_iota(jnp.int32, (fields, count), 1)
    field = field - (field * 1639) // 65536 * FQ
    chosen = jnp.where(field == lax.broadcasted_iota(jnp.int32, (fields, count), 0), 1.0, 0.0).astype(BF)
    value = inverse + 1
    high = value // 64
    both = jnp.concatenate([high.astype(F32), (value - high * 64).astype(F32)], axis=0).astype(BF)
    spread = dot(both, chosen)
    spread = jnp.where(own, spread[:samples] * 64 + spread[samples:], 0.0)
    return jnp.sum(spread, axis=0, keepdims=True).astype(jnp.int32) - 1


class Tree:
    def __init__(self):
        self.sem = pltpu.get_barrier_semaphore()
        self.group, member = lax.axis_index("group"), lax.axis_index("member")
        self.x, self.rest = member // 16, member % 16
        top = self.group * 4 + self.x
        self.root = jnp.logical_and(top == 0, self.rest == 0)
        self.leader = jnp.logical_and(top != 0, self.rest == 0)

    def signal(self, group, member):
        pl.semaphore_signal(self.sem, inc=1, device_id=(group, member), device_id_type=MESH)

    def arrive(self):
        @pl.when(self.rest != 0)
        def _():
            self.signal(self.group, self.x * 16)

    def pass_up(self):
        @pl.when(self.leader)
        def _():
            pl.semaphore_wait(self.sem, 15)
            self.signal(0, 0)

    def turn(self):
        @pl.when(self.root)
        def _():
            pl.semaphore_wait(self.sem, 30)

            def tell(k, carry):
                self.signal(k // 4, (k % 4) * 16)
                return carry

            lax.fori_loop(1, 16, tell, 0)

    def release(self):
        @pl.when(jnp.logical_not(self.root))
        def _():
            pl.semaphore_wait(self.sem, 1)

        @pl.when(self.rest == 0)
        def _():
            def tell(k, carry):
                self.signal(self.group, self.x * 16 + k)
                return carry

            lax.fori_loop(1, 16, tell, 0)


def step_kernel(
    inv_ref, ids_ref, next_ref, table_ref, accum_ref,
    e_ref, c1_ref, c2_ref, c3_ref, w1_ref, w2_hbm, w3_hbm, w1b_ref,
    nt_ref, na_ref, answers_ref, starts_ref,
    hot, high, grad, grads, send, rows, found, ask_v, ask_s, rows_out, rows_in, answers_out, answers_in, own, table_in,
    w2_ref, w3_ref, filters_in, *scratch,
):
    tree = Tree()
    tree.arrive()
    filters = [
        pltpu.make_async_copy(w3_hbm, w3_ref, filters_in.at[0]),
        pltpu.make_async_copy(w2_hbm, w2_ref, filters_in.at[1]),
    ]
    for copy in filters:
        copy.start()
    table_copy = pltpu.make_async_copy(table_ref, nt_ref, table_in)
    table_copy.start()
    grad[...] = jnp.zeros_like(grad)
    ask_v[...] = jnp.zeros_like(ask_v)
    owners, width = send.shape[0], send.shape[2]
    rows_dev = table_ref.shape[0]
    me = lax.axis_index("group") * 64 + lax.axis_index("member")
    count, listed = grads.shape[0] * FQ, ids_ref.shape[1]
    positions = in_a_row(inv_ref[...], count)

    owner, within, inside = ranks(ids_ref[...], CAP, rows_dev)
    target = within * owners + owner
    ask_owner, ask_within, ask_inside = ranks(next_ref[...], RCAP, rows_dev)
    numbers = [
        by_owner(owner, within, inside, owners, CAP),
        by_owner(ask_owner, ask_within, ask_inside, owners, RCAP),
    ]
    send[:, CAP, :] = jnp.concatenate(numbers + [jnp.zeros((owners, width - 16), F32)], axis=1)
    before = ask_owner < lax.broadcasted_iota(jnp.int32, (owners, ask_owner.shape[1]), 0)
    starts = lax.dot_general(
        jnp.ones((16, ask_owner.shape[1]), BF), jnp.where(before, 1.0, 0.0).astype(BF),
        (((1,), (1,)), ((), ())), preferred_element_type=F32,
    )
    starts_ref[...] = starts[:8].astype(jnp.int32)

    def between(turn, turns):
        pl.when(turn == turns // 4)(tree.pass_up)
        pl.when(turn == turns // 2)(tree.turn)
        pl.when(turn == turns * 3 // 4)(tree.release)

    for copy in filters:
        copy.wait()
    cin_all(
        between, e_ref, c1_ref, c2_ref, c3_ref, w1_ref, w2_ref, w3_ref, w1b_ref, grads, *scratch
    )

    g = jnp.concatenate(halves(grads[...].reshape(count, width)), axis=1)
    merged = []
    for b in range(listed // 256):
        place = lax.broadcasted_iota(jnp.int32, (256, count), 0) + b * 256
        m = dot(jnp.where(place == positions, 1.0, 0.0).astype(BF), g)
        merged.append(m[:, :width] + m[:, width:])
    merged = jnp.concatenate(halves(jnp.concatenate(merged, axis=0)), axis=1)
    for c in range(CAP):
        place = lax.broadcasted_iota(jnp.int32, (owners, listed), 0) + c * owners
        m = dot(jnp.where(place == target, 1.0, 0.0).astype(BF), merged)
        send[:, c, :] = m[:, :width] + m[:, width:]
    rows[me] = send[me]

    peers = Peers()

    def send_rows(step, count=8):
        to, members = peers.at(step)
        for member in members[:count]:
            pltpu.make_async_remote_copy(
                src_ref=send.at[to * 64 + member], dst_ref=rows.at[me],
                send_sem=rows_out, recv_sem=rows_in.at[step // 8],
                device_id=(to, member), device_id_type=MESH,
            ).start()

    lax.fori_loop(0, peers.steps - 1, lambda step, carry: (send_rows(step), carry)[1], 0)
    send_rows(peers.steps - 1, 7)

    part = owners // CLASSES
    group = lax.axis_index("group")

    def arrived(c, count):
        origin = (group - outward(c, 2) + CLASSES) % CLASSES
        at = pl.ds(pl.multiple_of(origin * part, part), count)
        pltpu.make_async_copy(send.at[at], rows.at[at], rows_in.at[c]).wait()
        at = pl.ds(pl.multiple_of(origin * part, part), part)
        numbers = rows[at, CAP, :].T[:16, :part].astype(jnp.int32)
        ask_v[origin, :, :part] = jnp.clip(numbers, 0, rows_dev - 1)
        values = jnp.concatenate([rows[at, k, :] for k in range(CAP)], axis=0)
        row = jnp.concatenate([numbers[k : k + 1] for k in range(CAP)], axis=1)
        place = lax.broadcasted_iota(jnp.int32, (64, CAP * part), 0)
        high[...] = jnp.where(place == row // 64, 1.0, 0.0)
        low = jnp.where(place == row - row // 64 * 64, 1.0, 0.0).astype(BF)
        return jnp.concatenate(halves(values), axis=1), low.reshape(4, 16, CAP * part)

    def product(b, values, low):
        for k in range(16):
            one = jnp.broadcast_to(high[pl.ds(b * 16 + k, 1), :], (16, CAP * part)).astype(BF)
            hot[k * 64 : (k + 1) * 64, :] = (low * one[None]).reshape(64, CAP * part)
        s = dot(hot[...], values)
        return s[:, :width] + s[:, width:]

    blocks = rows_dev // 1024

    def add_class(c, carry):
        values, low = arrived(c, part)

        def block(b, carry):
            at = pl.ds(pl.multiple_of(b * 1024, 1024), 1024)
            s = product(b, values, low)
            grad[at, :] = grad[at, :] + s
            return carry

        lax.fori_loop(0, blocks, block, 0, unroll=2)
        return carry

    lax.fori_loop(0, CLASSES - 1, add_class, 0)
    values, low = arrived(CLASSES - 1, part - 1)
    to_scalars = pltpu.make_async_copy(ask_v, ask_s, own)
    to_scalars.start()
    table_copy.wait()
    lane = lax.broadcasted_iota(jnp.int32, (128, 128), 1)

    def update(b, carry):
        at = pl.ds(pl.multiple_of(b * 1024, 1024), 1024)
        g = grad[at, :] + product(b, values, low)
        grad[at, :] = g
        total = dot(jnp.concatenate(halves(g * g), axis=1), jnp.ones((2 * width, 128), BF))
        means = jnp.zeros((128, 128), F32)
        for r in range(8):
            means = jnp.where(lane == r, total[r * 128 : (r + 1) * 128] * (1 / width), means)
        few = pl.ds(pl.multiple_of(8 * b, 8), 8)
        na = accum_ref[few, :] + means.T[:8]
        na_ref[few, :] = na
        scale = RATE / (jnp.sqrt(na) + EPS)
        scale = jnp.concatenate([scale, jnp.zeros((120, 128), F32)], axis=0).T
        for r in range(8):
            at = pl.ds(pl.multiple_of(b * 1024 + r * 128, 128), 128)
            nt_ref[at, :] = nt_ref[at, :] - grad[at, :] * scale[:, r : r + 1]
        return carry

    lax.fori_loop(0, blocks, update, 0, unroll=True)
    to_scalars.wait()

    def gather(step):
        to, members = peers.at(step)
        for member in members:
            for t in range(RCAP):
                row = ask_s[to, 8 + t, member]
                found[to * 64 + member, t : t + 1, :] = nt_ref[pl.ds(row, 1), :]

    def send_answers(step, count=8):
        to, members = peers.at(step)
        for member in members[:count]:
            pltpu.make_async_remote_copy(
                src_ref=found.at[to * 64 + member], dst_ref=answers_ref.at[me],
                send_sem=answers_out, recv_sem=answers_in,
                device_id=(to, member), device_id_type=MESH,
            ).start()

    def both(step, carry):
        gather(step)
        send_answers(step - 1)
        return carry

    gather(0)
    lax.fori_loop(1, peers.steps, both, 0)
    send_answers(peers.steps - 1, 7)
    mine = pltpu.make_async_copy(found.at[me], answers_ref.at[me], own)
    mine.start()
    mine.wait()
    others = pl.ds(0, owners - 1)
    pltpu.make_async_copy(send.at[others], rows.at[others], rows_out).wait()
    pltpu.make_async_copy(found.at[others], answers_ref.at[others], answers_in).wait()
    pltpu.make_async_copy(found.at[others], answers_ref.at[others], answers_out).wait()


def step(inverse, unique_ids, next_ids, table, accum, operands):
    rows_dev, width = table.shape
    samples = inverse.shape[0]
    owners = lax.axis_size("group") * lax.axis_size("member")
    vmem, free = pl.BlockSpec(memory_space=pltpu.VMEM), pl.BlockSpec(memory_space=pl.ANY)
    return pl.pallas_call(
        step_kernel,
        in_specs=[vmem] * 3 + [free] + [vmem] * 6 + [free] * 2 + [vmem],
        out_specs=[vmem, vmem, vmem, vmem],
        out_shape=[
            pltpu.VMEM(table.shape, F32),
            pltpu.VMEM((rows_dev // 128, 128), F32),
            pltpu.VMEM((owners, RCAP, width), F32),
            pltpu.VMEM((8, owners), jnp.int32),
        ],
        scratch_shapes=[
            pltpu.VMEM((1024, CAP * owners // CLASSES), BF),
            pltpu.VMEM((64, CAP * owners // CLASSES), F32),
            pltpu.VMEM(table.shape, F32),
            pltpu.VMEM((samples, FQ, width), F32),
            pltpu.VMEM((owners, CAP + 1, width), F32),
            pltpu.VMEM((owners, CAP + 1, width), F32),
            pltpu.VMEM((owners, RCAP, width), F32),
            pltpu.VMEM((CLASSES, 16, 128), jnp.int32),
            pltpu.SMEM((CLASSES, 16, 128), jnp.int32),
            pltpu.SemaphoreType.DMA,
            pltpu.SemaphoreType.DMA((CLASSES,)),
        ]
        + [pltpu.SemaphoreType.DMA] * 4
        + [pltpu.VMEM(w.shape, BF) for w in operands[5:7]]
        + [pltpu.SemaphoreType.DMA((2,))]
        + cin_scratch(samples),
        compiler_params=pltpu.CompilerParams(
            collective_id=0, has_side_effects=True, vmem_limit_bytes=56 << 20
        ),
        name="step",
    )(inverse, unique_ids, next_ids, table, accum.reshape(rows_dev // 128, 128), *operands)


def finish_kernel(starts_ref, answers_ref, nt_ref, na_ref, out_ref, nt_out, na_out, lines, starts, sems):
    scalars = pltpu.make_async_copy(starts_ref, starts, sems.at[2])
    scalars.start()
    table = pltpu.make_async_copy(nt_ref, nt_out, sems.at[0])
    table.start()
    na_out[...] = na_ref[...]
    scalars.wait()

    def place(k, carry):
        for t in range(16):
            o = k * 16 + t
            lines[pl.ds(starts[0, o], RCAP), :] = answers_ref[o]
        return carry

    lax.fori_loop(0, answers_ref.shape[0] // 16, place, 0)
    result = pltpu.make_async_copy(lines.at[pl.ds(0, out_ref.shape[0])], out_ref, sems.at[1])
    result.start()
    table.wait()
    result.wait()


def finish(starts, answers, new_table, new_accum, asked):
    vmem, free = pl.BlockSpec(memory_space=pltpu.VMEM), pl.BlockSpec(memory_space=pl.ANY)
    width = answers.shape[2]
    return pl.pallas_call(
        finish_kernel,
        in_specs=[vmem] * 4,
        out_specs=[free, free, vmem],
        out_shape=[
            jax.ShapeDtypeStruct((asked, width), F32),
            jax.ShapeDtypeStruct(new_table.shape, F32),
            jax.ShapeDtypeStruct(new_accum.shape, F32),
        ],
        scratch_shapes=[
            pltpu.VMEM((asked + RCAP, width), F32),
            pltpu.SMEM(starts.shape, jnp.int32),
            pltpu.SemaphoreType.DMA((3,)),
        ],
        compiler_params=pltpu.CompilerParams(vmem_limit_bytes=8 << 20),
        name="finish",
    )(starts, answers, new_table, new_accum)


def local(
    embeddings,
    cot_first,
    cot_second,
    cot_third,
    w_first,
    w_second,
    w_third,
    unique_ids,
    inverse,
    table,
    accum,
    next_ids,
):
    operands = cin_operands(embeddings, cot_first, cot_second, cot_third, w_first, w_second, w_third)
    new_table, new_accum, answers, starts = step(inverse, unique_ids, next_ids, table, accum, operands)
    returned, new_table, new_accum = finish(starts, answers, new_table, new_accum, next_ids.shape[1])
    return (new_table, new_accum.reshape(accum.shape), returned[None])


def solution(mesh):
    in_specs = (
        P(("group", "member"), None, None),
        P(("group", "member"), None),
        P(("group", "member"), None),
        P(("group", "member"), None),
        P(),
        P(),
        P(),
        P(("group", "member"), None),
        P(("group", "member"), None),
        P(("group", "member"), None),
        P(("group", "member")),
        P(("group", "member"), None),
    )
    out_specs = (
        P(("group", "member"), None),
        P(("group", "member")),
        P(("group", "member"), None, None),
    )
    return jax.shard_map(local, mesh=mesh, in_specs=in_specs, out_specs=out_specs, check_vma=False)
```
